128 devices in a mesh: seq: 16 (over z, y_hi, core), tensor: 8 (over x, y_lo).
Axes of the slice: x: 4, y: 4 (y_hi: 2, y_lo: 2; y = y_hi * 2 + y_lo), z: 4, core: 2. Of those that a mesh axis runs over, the one named last changes fastest.
Arguments:
- queries: bfloat16 [3, 48, 40, 5120], P(None, 'seq', None, 'tensor'), may hold values from -16 to 16
- keys_values: bfloat16 [2, 3, 48, 40, 5120], P(None, None, 'seq', None, 'tensor'), may hold values from -16 to 16
- out_weight: bfloat16 [5120, 5120], P('tensor'), may hold values from -0.078125 to 0.078125
- grad_out: bfloat16 [3, 48, 40, 5120], P(None, 'seq', 'tensor'), may hold values from -6 to 6
- window: int32 [40, 3], P('tensor'), may hold values from 0 to 3, as said below
- block_mask: int32 [1, 16, 5, 63], replicated, may hold values from 0 to 1, as said below
Outputs:
- layer_out: bfloat16 [3, 48, 40, 5120], P(None, 'seq', 'tensor')
- grad_queries: bfloat16 [3, 48, 40, 5120], P(None, 'seq', None, 'tensor')
- grad_keys_values: bfloat16 [2, 3, 48, 40, 5120], P(None, None, 'seq', None, 'tensor')
- grad_weight: bfloat16 [5120, 5120], P('tensor', 'seq')
The draws below stay inside these ranges and needn't reach their ends.
Inputs may be any that keep to these rules, and one draw needn't show every extreme that they name: `window`: in every group of 5 consecutive heads one head has the reach (1, 1, 3). `block_mask`: the middle entry of every tile's row (the tile itself) is 1.
All inputs are finite; a program needn't handle non-finite values.
Results may differ from the reference program's by a relative error of at most 0.014.
Values may be sent and summed in bfloat16 or wider, within the bound.
No kernel may reach another device: no remote copies, remote signals or barrier semaphores. Data moves between devices by JAX's collectives and lax.ppermute only.
A program may use at most 128 MiB of HBM per device.

```python
import jax
import jax.numpy as jnp
from jax import lax

D = 5120
HEADS = 40
HEAD_DIM = 128
FRAMES = 3
COLUMNS = 40
TILE_F = 3
TILE_H = 3
TILE_W = 8
REACH_F = 1
REACH_H = 1
REACH_W = 3
OFFSETS = 63
HEADS_DEV = 5
HEIGHT = 48
FRAME_TILES = 1
ROW_TILES = 16
COL_TILES = 5
N_SEQ = 16
N_TENSOR = 8


def base_values(key, salt):
    folded = jax.random.fold_in(key, salt)
    shape = (FRAMES, HEIGHT, COLUMNS, D)
    return jnp.clip(jax.random.normal(jax.random.fold_in(folded, 3), shape, jnp.float32), -6.0, 6.0)


def draw_queries(key, part):
    drawn_draw = base_values(key, 1)
    return drawn_draw.astype(jnp.bfloat16)


def draw_keys_values(key, part):
    key_draw = base_values(key, 2)
    values = base_values(key, 3)
    return jnp.stack([key_draw, values]).astype(jnp.bfloat16)


def draw_window(key, part):
    reaches = jnp.stack([jax.random.randint(jax.random.fold_in(key, 1), (HEADS,), 0, REACH_F + 1), jax.random.randint(jax.random.fold_in(key, 2), (HEADS,), 0, REACH_H + 1), jax.random.randint(jax.random.fold_in(key, 3), (HEADS,), 0, REACH_W + 1)], axis=1)
    chosen_slot = jax.random.randint(jax.random.fold_in(key, 4), (HEADS // HEADS_DEV,), 0, HEADS_DEV)
    head_slots = jnp.arange(HEADS, dtype=jnp.int32)
    chosen = head_slots % HEADS_DEV == jnp.repeat(chosen_slot, HEADS_DEV)
    widest = jnp.array([REACH_F, REACH_H, REACH_W], jnp.int32)
    return jnp.where(chosen[:, None], widest[None, :], reaches).astype(jnp.int32)


def draw_block_mask(key, part):
    mask_bits = jax.random.randint(jax.random.fold_in(key, 5), (FRAME_TILES, ROW_TILES, COL_TILES, OFFSETS), 0, 2)
    middle = jnp.arange(OFFSETS, dtype=jnp.int32) == OFFSETS // 2
    return jnp.where(middle, 1, mask_bits).astype(jnp.int32)


def raised(drawn, key, source, target, parts, factor):
    def block_of(axis_at):
        return (jnp.arange(drawn.shape[axis_at]) // (drawn.shape[axis_at] // parts)).reshape((-1,) + (1,) * (drawn.ndim - 1 - axis_at))

    one_side = jax.random.permutation(key, parts)[block_of(target)]
    other_side = (block_of(target) + parts // 2) % parts
    return jnp.where((block_of(source) == one_side) | (block_of(source) == other_side), factor * drawn, drawn)


def levels(key, dims, split, smallest, high):
    factor_of, own = 1.0, jax.random.fold_in(key, 6)
    for axis_at, blocks in split:
        steps = jnp.exp(jax.random.uniform(jax.random.fold_in(own, axis_at), (blocks,), jnp.float32, smallest / len(split), high / len(split)))
        factor_of = factor_of * jnp.repeat(steps, dims[axis_at] // blocks).reshape([-1 if axis == axis_at else 1 for axis in range(len(dims))])
    return factor_of


def gaussian(key, shape, width, limit, split=(), kind=jnp.bfloat16):
    result = jax.random.normal(key, shape, jnp.float32) * width
    if len(split) > 0:
        result = levels(key, shape, split, -0.22, 0.18) * result
    return jnp.clip(result, min=-limit, max=limit).astype(kind)


def heavy_noise(rng, extent, scale, reach, shards, heavy, kind=jnp.bfloat16):
    entries = scale * jax.random.normal(rng, extent, jnp.float32)
    if shards:
        entries = entries * levels(rng, extent, shards, -0.22, 0.18)
    return jnp.clip(raised(entries, jax.random.fold_in(rng, 3), *heavy), -reach, reach).astype(kind)


def setup_inputs(seed: int = 0) -> dict:
    splits = jax.random.split(jax.random.key(seed), 7)
    return {
        "queries": draw_queries(jax.random.fold_in(splits[6], 71), 0),
        "keys_values": draw_keys_values(jax.random.fold_in(splits[6], 71), 0),
        "out_weight": gaussian(splits[2], (D, D), D ** -0.5, 0.078125, ((0, 8),)),
        "grad_out": heavy_noise(splits[3], (FRAMES, HEIGHT, COLUMNS, D), 1.0, 6.0, ((1, 16), (2, 8)), (1, 3, 16, 2.0)),
        "window": draw_window(jax.random.fold_in(splits[6], 71), 0),
        "block_mask": draw_block_mask(jax.random.fold_in(splits[6], 71), 0),
    }


def product(left, right):
    return jnp.dot(left.astype(jnp.float32), right.astype(jnp.float32), preferred_element_type=jnp.float32)


def tile_order(grid):
    frames, height, columns, channels = grid.shape
    shaped = grid.reshape(frames // TILE_F, TILE_F, height // TILE_H, TILE_H, columns // TILE_W, TILE_W, channels)
    return shaped.transpose(0, 2, 4, 1, 3, 5, 6).reshape(-1, channels)


def grid_order(flat_rows, frames, height, columns):
    channels = flat_rows.shape[-1]
    shaped = flat_rows.reshape(frames // TILE_F, height // TILE_H, columns // TILE_W, TILE_F, TILE_H, TILE_W, channels)
    return shaped.transpose(0, 3, 1, 4, 2, 5, 6).reshape(frames, height, columns, channels)


def tile_coords(frames, height, columns, first_row):
    frame_count = frames // TILE_F
    row_count = height // TILE_H
    column_count = columns // TILE_W
    linear = jnp.arange(frame_count * row_count * column_count, dtype=jnp.int32)
    return (linear // (row_count * column_count), linear // column_count % row_count + first_row, linear % column_count)


def allowed_mask(reach_row, mask_rows, query_tiles, key_tiles, row_tiles):
    delta_f = key_tiles[0][None, :] - query_tiles[0][:, None]
    delta_h = key_tiles[1][None, :] - query_tiles[1][:, None]
    delta_w = key_tiles[2][None, :] - query_tiles[2][:, None]
    inside = (jnp.abs(delta_f) <= reach_row[0]) & (jnp.abs(delta_h) <= reach_row[1]) & (jnp.abs(delta_w) <= reach_row[2])
    inside = inside & ((key_tiles[1] >= 0) & (key_tiles[1] < row_tiles))[None, :]
    offset = ((delta_f + REACH_F) * (2 * REACH_H + 1) + delta_h + REACH_H) * (2 * REACH_W + 1) + delta_w + REACH_W
    mask_bits = jnp.sum(jnp.where(offset[:, :, None] == jnp.arange(OFFSETS, dtype=jnp.int32), mask_rows[:, None, :], 0), axis=-1)
    tiles_ok = inside & (mask_bits > 0)
    tile_size = TILE_F * TILE_H * TILE_W
    query_count, key_count = tiles_ok.shape
    spread = jnp.broadcast_to(tiles_ok[:, None, :, None], (query_count, tile_size, key_count, tile_size))
    return spread.reshape(query_count * tile_size, key_count * tile_size)


def head_forward(q_rows, k_rows, v_rows, allowed):
    scores = product(q_rows, k_rows.T) * HEAD_DIM ** -0.5
    scores = jnp.where(allowed, scores, -jnp.inf)
    row_max = jnp.max(scores, axis=1)
    weights = jnp.exp(scores - row_max[:, None])
    row_sum = jnp.sum(weights, axis=1)
    probs = weights / row_sum[:, None]
    attended = product(probs.astype(jnp.bfloat16), v_rows).astype(jnp.bfloat16)
    return attended, row_max, row_sum


def head_backward(q_rows, k_rows, v_rows, grad_rows, allowed, row_max, row_sum):
    scores = product(q_rows, k_rows.T) * HEAD_DIM ** -0.5
    scores = jnp.where(allowed, scores, -jnp.inf)
    probs = jnp.exp(scores - row_max[:, None]) / row_sum[:, None]
    rounded = probs.astype(jnp.bfloat16)
    grad_values = product(rounded.T, grad_rows)
    grad_probs = product(grad_rows, v_rows.T)
    row_delta = jnp.sum(probs * grad_probs, axis=1)
    grad_scores = (probs * (grad_probs - row_delta[:, None]) * HEAD_DIM ** -0.5).astype(jnp.bfloat16)
    return product(grad_scores, k_rows), product(grad_scores.T, q_rows), grad_values


def reference(queries, keys_values, out_weight, grad_out, window, block_mask):
    frames, height, columns, model_width = queries.shape
    padded_kv = jnp.pad(keys_values, ((0, 0), (0, 0), (TILE_H, TILE_H), (0, 0), (0, 0)))
    row_list = jnp.arange(N_SEQ, dtype=jnp.int32)
    head_list = jnp.arange(HEADS, dtype=jnp.int32)
    zero_index = jnp.zeros((), jnp.int32)

    def gather_rows(row_index, head_index):
        first_row = (row_index * TILE_H).astype(jnp.int32)
        first_chan = (head_index * HEAD_DIM).astype(jnp.int32)
        q_rows = tile_order(lax.dynamic_slice(queries, (zero_index, first_row, zero_index, first_chan), (frames, TILE_H, columns, HEAD_DIM)))
        kv_rows = lax.dynamic_slice(padded_kv, (zero_index, zero_index, first_row, zero_index, first_chan), (2, frames, 3 * TILE_H, columns, HEAD_DIM))
        mask_rows = lax.dynamic_slice_in_dim(block_mask, row_index.astype(jnp.int32), 1, 1).reshape(-1, OFFSETS)
        allowed = allowed_mask(window[head_index], mask_rows, tile_coords(frames, TILE_H, columns, row_index), tile_coords(frames, 3 * TILE_H, columns, row_index - 1), N_SEQ)
        return q_rows, tile_order(kv_rows[0]), tile_order(kv_rows[1]), allowed

    def forward_head(head_index):
        def forward_row(row_index):
            q_rows, k_rows, v_rows, allowed = gather_rows(row_index, head_index)
            return head_forward(q_rows, k_rows, v_rows, allowed)
        return lax.map(forward_row, row_list)

    attended, row_max, row_sum = lax.map(forward_head, head_list)
    joined = attended.transpose(1, 2, 0, 3).reshape(N_SEQ, -1, model_width)

    def regrid(flat_rows):
        return grid_order(flat_rows, frames, TILE_H, columns)

    attn_grid = jax.vmap(regrid)(joined).transpose(1, 0, 2, 3, 4).reshape(frames, height, columns, model_width)
    attn_flat = attn_grid.reshape(-1, model_width)
    group_width = model_width // N_TENSOR
    mixed = jnp.zeros((attn_flat.shape[0], model_width), jnp.float32)
    for group in range(N_TENSOR):
        partial_value = product(attn_flat[:, group * group_width:(group + 1) * group_width], out_weight[group * group_width:(group + 1) * group_width]).astype(jnp.bfloat16)
        mixed = mixed + lax.optimization_barrier(partial_value).astype(jnp.float32)
    layer_out = mixed.astype(jnp.bfloat16).reshape(frames, height, columns, model_width)

    grad_flat = grad_out.reshape(-1, model_width)
    grad_attn = product(grad_flat, out_weight.T).astype(jnp.bfloat16).reshape(frames, height, columns, model_width)

    def add_row(row_index, carried):
        first_row = (row_index * TILE_H).astype(jnp.int32)
        attn_rows = lax.dynamic_slice_in_dim(attn_grid, first_row, TILE_H, 1).reshape(-1, model_width)
        grad_rows = lax.dynamic_slice_in_dim(grad_out, first_row, TILE_H, 1).reshape(-1, model_width)
        partial_value = product(attn_rows.T, grad_rows).astype(jnp.bfloat16)
        return carried + lax.optimization_barrier(partial_value).astype(jnp.float32)

    grad_weight = lax.fori_loop(0, N_SEQ, add_row, jnp.zeros((model_width, model_width), jnp.float32)).astype(jnp.bfloat16)

    def backward_head(inputs):
        head_index, head_max, head_sum = inputs

        def backward_row(carried, row_inputs):
            row_index, row_top, row_total = row_inputs
            q_rows, k_rows, v_rows, allowed = gather_rows(row_index, head_index)
            first_row = (row_index * TILE_H).astype(jnp.int32)
            first_chan = (head_index * HEAD_DIM).astype(jnp.int32)
            grad_rows = tile_order(lax.dynamic_slice(grad_attn, (zero_index, first_row, zero_index, first_chan), (frames, TILE_H, columns, HEAD_DIM)))
            grad_q, grad_k, grad_v = head_backward(q_rows, k_rows, v_rows, grad_rows, allowed, row_top, row_total)
            both = jnp.stack([grid_order(grad_k, frames, 3 * TILE_H, columns), grid_order(grad_v, frames, 3 * TILE_H, columns)])
            current = lax.dynamic_slice_in_dim(carried, first_row, 3 * TILE_H, 2)
            carried = lax.dynamic_update_slice_in_dim(carried, current + both, first_row, 2)
            return carried, grid_order(grad_q, frames, TILE_H, columns)

        initial = jnp.zeros((2, frames, height + 2 * TILE_H, columns, HEAD_DIM), jnp.float32)
        carried, grad_q = lax.scan(backward_row, initial, (row_list, head_max, head_sum))
        return carried[:, :, TILE_H:TILE_H + height], grad_q

    grad_kv, grad_q = lax.map(backward_head, (head_list, row_max, row_sum))
    grad_keys_values = grad_kv.transpose(1, 2, 3, 4, 0, 5).reshape(2, frames, height, columns, model_width).astype(jnp.bfloat16)
    grad_queries = grad_q.transpose(2, 1, 3, 4, 0, 5).reshape(frames, height, columns, model_width).astype(jnp.bfloat16)
    return (layer_out, grad_queries, grad_keys_values, grad_weight)
```

```python
import functools

import jax
import jax.numpy as jnp
import numpy as np
from jax import lax
from jax.experimental import pallas as pl
from jax.experimental.pallas import tpu as pltpu
from jax.sharding import PartitionSpec as P

HEAD_DIM = 128
TILE_W = 8
REACH_W = 3
OFFSETS = 63
SCALE = HEAD_DIM ** (-0.5)
OUTSIDE = -1e30
F32 = jnp.float32
BF16 = jnp.bfloat16


def dot(a, b, dims):
    return lax.dot_general(a, b, (dims, ((), ())), preferred_element_type=F32)


def tensor_shift(value, dx, dy):
    pairs = [
        (x * 2 + y, (x + dx) % 4 * 2 + (y + dy) % 2) for x in range(4) for y in range(2)
    ]
    return lax.ppermute(value, "tensor", pairs)


def seq_shift(value, dz, dy, core=0):
    pairs = [
        ((z * 2 + y) * 2 + c, ((z + dz) % 4 * 2 + (y + dy) % 2) * 2 + (c + core) % 2)
        for z in range(4)
        for y in range(2)
        for c in range(2)
    ]
    return lax.ppermute(value, "seq", pairs)


def added(*terms):
    total = terms[0].astype(F32)
    for term in terms[1:]:
        total = total + term.astype(F32)
    return total


def gathered(own, shift):
    half = own.shape[0] // 2
    c01 = shift(own, 0, 1)
    c10 = shift(own, -1, 0)
    c30 = shift(own, 1, 0)
    c11 = shift(c01, -1, 0)
    c31 = shift(c01, 1, 0)
    c20 = [shift(c10[:half], -1, 0), shift(c30[half:], 1, 0)]
    c21 = [shift(c11[:half], -1, 0), shift(c31[half:], 1, 0)]
    return jnp.concatenate([own, c01, c10, c11, *c20, *c21, c30, c31], axis=0)


def scattered(block, half, shift):
    arrived = {}
    for e in (1, 0):
        far = block(2, e)
        arrived[1, e] = shift(far[:half], 1, 0)
        arrived[3, e] = shift(far[half:], -1, 0)
    near = {}
    for e in (1, 0):
        up, down = block(1, e), block(3, e)
        up = jnp.concatenate([added(up[:half], arrived[1, e]).astype(BF16), up[half:]])
        down = jnp.concatenate([down[:half], added(down[half:], arrived[3, e]).astype(BF16)])
        near[1, e] = shift(up, 1, 0)
        near[3, e] = shift(down, -1, 0)
    side = shift(added(block(0, 1), near[1, 1], near[3, 1]).astype(BF16), 0, 1)
    return block(0, 0), near[1, 0], near[3, 0], side


def forward_kernel(q_ref, own_ref, up_ref, down_ref, bias_ref, hot_ref, perm_ref, p_ref, att_ref):
    qa = jnp.concatenate([q_ref[...], hot_ref[...]], axis=1)
    scores = []
    for b, ref in enumerate((up_ref, own_ref, down_ref)):
        bias = jnp.concatenate([bias_ref[0, b]] * 9, axis=0).astype(BF16)
        ka = jnp.concatenate([ref[0], bias], axis=1)
        scores.append(dot(ka, qa, ((1,), (1,))))
    top = jnp.max(scores[0], axis=0, keepdims=True)
    for s in scores[1:]:
        top = jnp.maximum(top, jnp.max(s, axis=0, keepdims=True))
    weights = [jnp.exp((s - top) * SCALE) for s in scores]
    total = jnp.sum(weights[0], axis=0, keepdims=True)
    for w in weights[1:]:
        total = total + jnp.sum(w, axis=0, keepdims=True)
    inverse = 1.0 / total
    attended = None
    for b, ref in enumerate((up_ref, own_ref, down_ref)):
        probs = (weights[b] * inverse).astype(BF16)
        p_ref[0, b] = probs
        part = dot(ref[1], probs, ((0,), (0,)))
        attended = part if attended is None else attended + part
    att_ref[...] = dot(perm_ref[...], attended.astype(BF16), ((1,), (1,))).astype(BF16)


def backward_kernel(
    q_ref, own_ref, up_ref, down_ref, p_ref, ga_ref, perm_ref, gq_ref, gown_ref, gup_ref, gdown_ref
):
    q = q_ref[...]
    g = dot(perm_ref[...], ga_ref[...], ((1,), (0,))).astype(BF16)
    refs = (up_ref, own_ref, down_ref)
    outs = (gup_ref, gown_ref, gdown_ref)
    grads = []
    delta = None
    for b in range(3):
        gp = dot(refs[b][1], g, ((1,), (1,)))
        part = jnp.sum(p_ref[0, b].astype(F32) * gp, axis=0, keepdims=True)
        delta = part if delta is None else delta + part
        grads.append(gp)
    gq = None
    for b in range(3):
        probs = p_ref[0, b]
        ds = (probs.astype(F32) * (grads[b] - delta) * SCALE).astype(BF16)
        outs[b][0] = dot(ds, q, ((1,), (0,))).astype(outs[b].dtype)
        outs[b][1] = dot(probs, g, ((1,), (0,))).astype(outs[b].dtype)
        part = dot(refs[b][0], ds, ((0,), (0,)))
        gq = part if gq is None else gq + part
    gq_ref[...] = gq.T.astype(BF16)


def weight_kernel(order_ref, g_ref, att_ref, keep_ref, send_ref):
    grad = dot(g_ref[...], att_ref[...], ((0,), (0,)))
    half = keep_ref.shape[1]
    low, high = grad[:half], grad[half:]
    first = order_ref[8] == 0
    keep_ref[0] = jnp.where(first, low, high).astype(BF16)
    send_ref[0] = jnp.where(first, high, low).astype(BF16)


def turned_kernel(a_ref, b_ref, c_ref, d_ref, out_ref):
    out_ref[...] = added(a_ref[...], b_ref[...], c_ref[...], d_ref[...]).T.astype(BF16)


def mask_bias(window, own_mask, seq_place, row_tiles):
    heads = window.shape[0]
    columns = own_mask.shape[0]
    rows = own_mask.reshape(columns, 3, 3, 7)[:, 1]
    query = np.arange(columns)
    delta = query[:, None] - query[None, :]
    pick = (delta[:, :, None] + REACH_W == np.arange(7)).astype(np.int32)
    bits = jnp.sum(rows.transpose(1, 0, 2)[:, None] * pick[None], axis=-1)
    dh = jnp.arange(3, dtype=jnp.int32) - 1
    tile_row = dh + seq_place
    row_ok = (tile_row >= 0) & (tile_row < row_tiles)
    inside = (jnp.abs(dh)[None, :] <= window[:, 1:2]) & row_ok[None, :] & (window[:, :1] >= 0)
    near = np.abs(delta)[None] <= window[:, 2][:, None, None]
    ok = inside[:, :, None, None] & near[:, None] & (bits > 0)[None]
    bias = jnp.where(ok, 0.0, OUTSIDE).astype(F32)
    bias = jnp.pad(bias, ((0, 0), (0, 0), (0, 0), (0, 128 - columns)))
    wide = jnp.broadcast_to(bias[:, :, :, None], (heads, 3, columns, TILE_W, 128))
    return wide.reshape(heads, 3, columns * TILE_W, 128)


def shards(queries, keys_values, out_weight, grad_out, window, block_mask):
    frames, tile_rows, columns, channels = queries.shape
    model_width = grad_out.shape[3]
    local_columns = grad_out.shape[2]
    tokens = frames * tile_rows * columns
    heads = channels // HEAD_DIM
    strips = frames * tile_rows
    row_tiles = lax.axis_size("seq")
    seq_place = lax.axis_index("seq")
    tensor_place = lax.axis_index("tensor")
    spot_z, spot_y, core = seq_place // 4, seq_place // 2 % 2, seq_place % 2
    spot_x, spot_low = tensor_place // 2, tensor_place % 2

    up = lax.ppermute(keys_values, "seq", [(i, i + 1) for i in range(row_tiles - 1)])
    down = lax.ppermute(keys_values, "seq", [(i + 1, i) for i in range(row_tiles - 1)])

    piece = strips * local_columns
    room = -(-piece // 16) * 16
    own_grad = jnp.pad(grad_out.reshape(piece, model_width), ((0, room - piece), (0, 0)))
    all_grad = gathered(own_grad, tensor_shift)
    slots = 8 * room

    slot = lax.iota(jnp.int32, slots)
    block, row = slot // room, slot % room
    owner = (spot_x + block // 2) % 4 * 2 + (spot_low + block % 2) % 2
    place = row // local_columns * columns + owner * local_columns + row % local_columns
    place = jnp.where(row < piece, place, -1)
    cell = lax.iota(jnp.int32, tokens)
    perm = (place[:, None] == cell[None, :]).astype(BF16)
    perm_back = (cell[:, None] == place[None, :]).astype(BF16)
    hot = (cell[:, None] % columns // TILE_W == lax.iota(jnp.int32, 128)[None, :]).astype(BF16)

    own_mask = lax.dynamic_slice_in_dim(block_mask, seq_place, 1, 1).reshape(-1, OFFSETS)
    bias = mask_bias(window, own_mask, seq_place, row_tiles)

    flat_q = queries.reshape(tokens, channels)
    flat = [v.reshape(2, tokens, channels) for v in (keys_values, up, down)]
    q_spec = pl.BlockSpec((tokens, HEAD_DIM), lambda h: (0, h))
    kv_spec = pl.BlockSpec((2, tokens, HEAD_DIM), lambda h: (0, 0, h))
    p_spec = pl.BlockSpec((1, 3, tokens, tokens), lambda h: (h, 0, 0, 0))
    slot_spec = pl.BlockSpec((slots, HEAD_DIM), lambda h: (0, h))

    def whole(shape):
        return pl.BlockSpec(shape, lambda h: (0,) * len(shape))

    pairs = heads * tokens * 3 * tokens
    probs, attended = pl.pallas_call(
        forward_kernel,
        grid=(heads,),
        in_specs=[
            q_spec,
            kv_spec,
            kv_spec,
            kv_spec,
            pl.BlockSpec((1, 3, columns, 128), lambda h: (h, 0, 0, 0)),
            whole((tokens, 128)),
            whole((slots, tokens)),
        ],
        out_specs=[p_spec, slot_spec],
        out_shape=[
            jax.ShapeDtypeStruct((heads, 3, tokens, tokens), BF16),
            jax.ShapeDtypeStruct((slots, channels), BF16),
        ],
        cost_estimate=pl.CostEstimate(
            flops=pairs * 768, transcendentals=pairs, bytes_accessed=8 << 20
        ),
        name="attend",
    )(flat_q, *flat, bias, hot, perm)

    mixed = jnp.dot(attended, out_weight, preferred_element_type=F32).astype(BF16)
    grad_attn = lax.dot_general(
        all_grad, out_weight, (((1,), (1,)), ((), ())), preferred_element_type=F32
    ).astype(BF16)

    step = lax.iota(jnp.int32, 8)
    chips = (spot_z + step // 2) % 4 * 2 + (spot_y + step % 2) % 2
    order = jnp.concatenate([chips, core[None]]).astype(jnp.int32)
    wide = model_width // 8
    keep, send = pl.pallas_call(
        weight_kernel,
        grid_spec=pltpu.PrefetchScalarGridSpec(
            num_scalar_prefetch=1,
            grid=(8,),
            in_specs=[
                pl.BlockSpec((slots, wide), lambda i, o: (0, o[i])),
                pl.BlockSpec((slots, channels), lambda i, o: (0, 0)),
            ],
            out_specs=[pl.BlockSpec((1, wide // 2, channels), lambda i, o: (i, 0, 0))] * 2,
        ),
        out_shape=[jax.ShapeDtypeStruct((8, wide // 2, channels), BF16)] * 2,
        cost_estimate=pl.CostEstimate(
            flops=2 * slots * model_width * channels, transcendentals=0, bytes_accessed=12 << 20
        ),
        name="weight",
    )(order, all_grad, attended)
    both = added(keep, seq_shift(send, 0, 0, 1)).astype(BF16)
    weight_terms = scattered(lambda d, e: both[d * 2 + e], wide // 4, seq_shift)
    grad_weight = pl.pallas_call(
        turned_kernel,
        out_shape=jax.ShapeDtypeStruct((channels, wide // 2), BF16),
        name="turned",
    )(*weight_terms)

    mixed_terms = scattered(
        lambda d, e: mixed[(d * 2 + e) * room : (d * 2 + e + 1) * room], room // 2, tensor_shift
    )
    layer_out = (
        added(*mixed_terms)[:piece]
        .astype(BF16)
        .reshape(frames, tile_rows, local_columns, model_width)
    )

    grad_q, grad_own, grad_up, grad_down = pl.pallas_call(
        backward_kernel,
        grid=(heads,),
        in_specs=[
            q_spec,
            kv_spec,
            kv_spec,
            kv_spec,
            p_spec,
            slot_spec,
            whole((tokens, slots)),
        ],
        out_specs=[q_spec, kv_spec, kv_spec, kv_spec],
        out_shape=[
            jax.ShapeDtypeStruct((tokens, channels), BF16),
            jax.ShapeDtypeStruct((2, tokens, channels), F32),
            jax.ShapeDtypeStruct((2, tokens, channels), BF16),
            jax.ShapeDtypeStruct((2, tokens, channels), BF16),
        ],
        cost_estimate=pl.CostEstimate(
            flops=pairs * 1024, transcendentals=0, bytes_accessed=12 << 20
        ),
        name="differentiate",
    )(flat_q, *flat, probs, grad_attn, perm_back)

    from_below = lax.ppermute(grad_up, "seq", [(i + 1, i) for i in range(row_tiles - 1)])
    from_above = lax.ppermute(grad_down, "seq", [(i, i + 1) for i in range(row_tiles - 1)])
    grad_kv = added(grad_own, from_below, from_above).astype(BF16)
    return (
        layer_out,
        grad_q.reshape(queries.shape),
        grad_kv.reshape(keys_values.shape),
        grad_weight,
    )


def solution(mesh):
    return jax.shard_map(
        shards,
        mesh=mesh,
        in_specs=(
            P(None, "seq", None, "tensor"),
            P(None, None, "seq", None, "tensor"),
            P("tensor", None),
            P(None, "seq", "tensor", None),
            P("tensor", None),
            P(),
        ),
        out_specs=(
            P(None, "seq", "tensor", None),
            P(None, "seq", None, "tensor"),
            P(None, None, "seq", None, "tensor"),
            P("tensor", "seq"),
        ),
        check_vma=False,
    )
```

```python
import jax
import jax.numpy as jnp
import numpy as np
from jax import lax
from jax.experimental import pallas as pl
from jax.experimental.pallas import tpu as pltpu
from jax.sharding import PartitionSpec as P

HEAD_DIM = 128
TILE_W = 8
REACH_W = 3
OFFSETS = 63
SCALE = HEAD_DIM ** (-0.5)
OUTSIDE = -1e30
F32 = jnp.float32
BF16 = jnp.bfloat16


def dot(a, b, dims):
    return lax.dot_general(a, b, (dims, ((), ())), preferred_element_type=F32)


def tensor_shift(value, dx, dy):
    pairs = [
        (x * 2 + y, (x + dx) % 4 * 2 + (y + dy) % 2) for x in range(4) for y in range(2)
    ]
    return lax.ppermute(value, "tensor", pairs)


def seq_shift(value, dz, dy, core=0):
    pairs = [
        ((z * 2 + y) * 2 + c, ((z + dz) % 4 * 2 + (y + dy) % 2) * 2 + (c + core) % 2)
        for z in range(4)
        for y in range(2)
        for c in range(2)
    ]
    return lax.ppermute(value, "seq", pairs)


def added(*terms):
    total = terms[0].astype(F32)
    for term in terms[1:]:
        total = total + term.astype(F32)
    return total


def tops(room):
    upper = room // 2 // 16 * 16
    return upper, room - upper


def gathered(own, shift):
    t0, t1 = tops(own.shape[0])
    c01 = shift(own, 0, 1)
    c10 = shift(own, -1, 0)
    c30 = shift(own, 1, 0)
    c11 = shift(c01, -1, 0)
    c31 = shift(c01, 1, 0)
    c20 = [shift(c10[:t0], -1, 0), shift(c30[t0:], 1, 0)]
    c21 = [shift(c11[:t1], -1, 0), shift(c31[t1:], 1, 0)]
    return [own, c01, c10, c11, *c20, *c21, c30, c31], (c11, c31)


ANYWHERE = pl.BlockSpec(memory_space=pl.ANY)


def kernel(body, outs, args, specs=None, out_specs=None, grid=(), after=(), flops=0, moved=0, scratch=()):
    count = len(args)

    def run(*refs):
        return body(*refs[:count], *refs[count + len(after) :])

    vector = pl.BlockSpec(memory_space=pltpu.VMEM)
    specs = [vector] * count if specs is None else specs
    out_specs = [vector] * len(outs) if out_specs is None else out_specs
    return pl.pallas_call(
        run,
        grid=grid,
        in_specs=[*specs, *[ANYWHERE] * len(after)],
        out_specs=out_specs,
        out_shape=[jax.ShapeDtypeStruct(shape, kind) for shape, kind in outs],
        scratch_shapes=scratch,
        cost_estimate=pl.CostEstimate(flops=flops, transcendentals=0, bytes_accessed=moved),
    )(*args, *after)


def join_total(zero_ref, plus_ref, minus_ref, plus_sum_ref, minus_sum_ref):
    upper, lower = plus_sum_ref.shape[0], minus_sum_ref.shape[0]
    first = added(zero_ref[:upper], plus_sum_ref[...], minus_ref[lower:])
    second = added(zero_ref[upper:], plus_ref[upper:], minus_sum_ref[...])
    return jnp.concatenate([first, second], axis=0)


def side_kernel(*refs):
    refs[-1][...] = join_total(*refs[:5]).astype(BF16)


def relay_kernel(kept_plus_ref, kept_minus_ref, plus_ref, minus_ref, plus_out, minus_out):
    plus_out[...] = added(kept_plus_ref[...], plus_ref[: plus_out.shape[0]]).astype(BF16)
    minus_out[...] = added(kept_minus_ref[...], minus_ref[: minus_out.shape[0]]).astype(BF16)


def mixed_kernel(*refs):
    out_ref = refs[-1]
    total = (join_total(*refs[:5]) + refs[5][...].astype(F32)).astype(BF16).astype(F32)
    rows = out_ref.shape[1]
    for i in range(out_ref.shape[0]):
        out_ref[i] = total[i * rows : (i + 1) * rows].astype(BF16)


def split_kernel(*refs):
    core_ref, mine_ref, other_ref = refs[6:]
    total = join_total(*refs[:5]) + refs[5][...].astype(F32)
    half = mine_ref.shape[1]
    low, high = total[:, :half], total[:, half:]
    first = core_ref[0] == 0
    mine_ref[...] = jnp.where(first, low, high).astype(BF16)
    other_ref[...] = jnp.where(first, high, low).astype(BF16)


def stack_kernel(mine_ref, came_ref, core_ref, out_ref):
    first = core_ref[0] == 0
    mine, came = mine_ref[...].astype(F32), came_ref[...].astype(F32)
    step = HEAD_DIM // 2
    for i in range(mine.shape[0] // step):
        rows = slice(i * step, (i + 1) * step)
        here = 2 * i * step
        out_ref[here : here + step] = jnp.where(first, mine[rows], came[rows]).astype(BF16)
        out_ref[here + step : here + 2 * step] = jnp.where(first, came[rows], mine[rows]).astype(BF16)


SCALAR = pl.BlockSpec(memory_space=pltpu.SMEM)
VECTOR = pl.BlockSpec(memory_space=pltpu.VMEM)


def hop(shift, arrays):
    return [shift(arrays[i], 1 - 2 * i, 0) for i in range(2)]


def forward_kernel(
    q_ref, own_ref, up_ref, down_ref, bias_ref, hot_ref, perm_ref, core_ref, p_ref, att_ref, turned_ref
):
    qa = jnp.concatenate([q_ref[...], hot_ref[...]], axis=1)
    scores = []
    for b, ref in enumerate((up_ref, own_ref, down_ref)):
        bias = jnp.concatenate([bias_ref[0, b]] * 9, axis=0).astype(BF16)
        ka = jnp.concatenate([ref[0], bias], axis=1)
        scores.append(dot(ka, qa, ((1,), (1,))))
    top = jnp.max(scores[0], axis=0, keepdims=True)
    for s in scores[1:]:
        top = jnp.maximum(top, jnp.max(s, axis=0, keepdims=True))
    weights = [jnp.exp((s - top) * SCALE) for s in scores]
    total = jnp.sum(weights[0], axis=0, keepdims=True)
    for w in weights[1:]:
        total = total + jnp.sum(w, axis=0, keepdims=True)
    inverse = 1.0 / total
    attended = None
    for b, ref in enumerate((up_ref, own_ref, down_ref)):
        probs = (weights[b] * inverse).astype(BF16)
        p_ref[0, b] = probs
        part = dot(ref[1], probs, ((0,), (0,)))
        attended = part if attended is None else attended + part
    attended = attended.astype(BF16)
    att_ref[...] = dot(perm_ref[...], attended, ((1,), (1,))).astype(BF16)
    turned = dot(attended, perm_ref[...], ((1,), (1,)))
    low, high = turned[: HEAD_DIM // 2], turned[HEAD_DIM // 2 :]
    first = core_ref[0] == 0
    turned_ref[0, 0] = jnp.where(first, low, high).astype(BF16)
    turned_ref[1, 0] = jnp.where(first, high, low).astype(BF16)


def backward_kernel(
    q_ref, own_ref, up_ref, down_ref, p_ref, ga_ref, perm_ref, gq_ref, gown_ref, gup_ref, gdown_ref
):
    q = q_ref[...]
    g = dot(perm_ref[...], ga_ref[...], ((1,), (0,))).astype(BF16)
    refs = (up_ref, own_ref, down_ref)
    outs = (gup_ref, gown_ref, gdown_ref)
    grads = []
    delta = None
    for b in range(3):
        gp = dot(refs[b][1], g, ((1,), (1,)))
        part = jnp.sum(p_ref[0, b].astype(F32) * gp, axis=0, keepdims=True)
        delta = part if delta is None else delta + part
        grads.append(gp)
    gq = None
    for b in range(3):
        probs = p_ref[0, b]
        ds = (probs.astype(F32) * (grads[b] - delta) * SCALE).astype(BF16)
        outs[b][0] = dot(ds, q, ((1,), (0,))).astype(outs[b].dtype)
        outs[b][1] = dot(probs, g, ((1,), (0,))).astype(outs[b].dtype)
        part = dot(refs[b][0], ds, ((0,), (0,)))
        gq = part if gq is None else gq + part
    gq_ref[...] = gq.T.astype(BF16)


def weight_kernel(order_ref, turned_ref, *refs):
    *pieces, after_ref, keep_ref, send_ref = refs
    g = jnp.concatenate([p[...] for p in pieces], axis=0)
    grad = dot(turned_ref[...], g, ((1,), (0,))).astype(BF16)
    half = keep_ref.shape[1]
    keep_ref[0] = grad[:half]
    send_ref[0] = grad[half:]


def place_parts(rows, room, upper, refs):
    plus, minus, kept_plus, kept_minus, zero = refs
    plus[...] = jnp.concatenate([rows(2, 0, upper), rows(1, upper, room)], axis=0).astype(BF16)
    minus[...] = jnp.concatenate([rows(2, upper, room), rows(3, 0, upper)], axis=0).astype(BF16)
    kept_plus[...] = rows(1, 0, upper).astype(BF16)
    kept_minus[...] = rows(3, upper, room).astype(BF16)
    zero[...] = rows(0, 0, room).astype(BF16)


def part_rows(room, upper):
    return [room, room, upper, room - upper, room]


def fold_kernel(keep_ref, came_ref, *outs):
    room = keep_ref.shape[1]

    def rows(d, start, end):
        return added(keep_ref[d, start:end], came_ref[d, start:end])

    place_parts(rows, room, outs[2].shape[0], outs)


def project_kernel(att_ref, w_ref, *outs):
    mixed = dot(att_ref[...], w_ref[...], ((1,), (0,)))
    room = outs[0].shape[0]
    for i, e in enumerate((1, 0)):
        refs = outs[5 * i : 5 * i + 5]

        def rows(d, start, end, e=e):
            base = (d * 2 + e) * room
            return mixed[base + start : base + end]

        place_parts(rows, room, refs[2].shape[0], refs)


def attn_grad_kernel(w_ref, *refs):
    *pieces, ga_ref, total_ref = refs
    step = pl.program_id(0)
    g = jnp.concatenate([p[...] for p in pieces], axis=0)
    part = dot(g, w_ref[...], ((1,), (1,)))

    @pl.when(step == 0)
    def _():
        total_ref[...] = part

    @pl.when(step > 0)
    def _():
        total_ref[...] += part

    @pl.when(step == pl.num_programs(0) - 1)
    def _():
        ga_ref[...] = total_ref[...].astype(BF16)


def total_kernel(*refs):
    out_ref = refs[-1]
    start = 0
    for i in range(0, len(refs) - 1, 3):
        part = added(refs[i][...], refs[i + 1][...], refs[i + 2][...]).astype(BF16)
        out_ref[:, :, start : start + part.shape[2]] = part
        start += part.shape[2]


def mask_bias(window, own_mask, seq_place, row_tiles):
    heads = window.shape[0]
    columns = own_mask.shape[0]
    rows = own_mask.reshape(columns, 3, 3, 7)[:, 1]
    query = np.arange(columns)
    delta = query[:, None] - query[None, :]
    pick = (delta[:, :, None] + REACH_W == np.arange(7)).astype(np.int32)
    bits = jnp.sum(rows.transpose(1, 0, 2)[:, None] * pick[None], axis=-1)
    dh = jnp.arange(3, dtype=jnp.int32) - 1
    tile_row = dh + seq_place
    row_ok = (tile_row >= 0) & (tile_row < row_tiles)
    inside = (jnp.abs(dh)[None, :] <= window[:, 1:2]) & row_ok[None, :] & (window[:, :1] >= 0)
    near = np.abs(delta)[None] <= window[:, 2][:, None, None]
    ok = inside[:, :, None, None] & near[:, None] & (bits > 0)[None]
    bias = jnp.where(ok, 0.0, OUTSIDE).astype(F32)
    bias = jnp.pad(bias, ((0, 0), (0, 0), (0, 0), (0, 128 - columns)))
    wide = jnp.broadcast_to(bias[:, :, :, None], (heads, 3, columns, TILE_W, 128))
    return wide.reshape(heads, 3, columns * TILE_W, 128)


def layer(queries, keys_values, out_weight, grad_out, window, block_mask):
    frames, tile_rows, columns, channels = queries.shape
    model_width = grad_out.shape[3]
    local_columns = grad_out.shape[2]
    tokens = frames * tile_rows * columns
    heads = channels // HEAD_DIM
    strips = frames * tile_rows
    row_tiles = lax.axis_size("seq")
    seq_place = lax.axis_index("seq")
    tensor_place = lax.axis_index("tensor")
    spot_z, spot_y, core = seq_place // 4, seq_place // 2 % 2, seq_place % 2
    spot_x, spot_low = tensor_place // 2, tensor_place % 2
    core = core[None].astype(jnp.int32)

    onward = [(i, i + 1) for i in range(row_tiles - 1)]
    back = [(i + 1, i) for i in range(row_tiles - 1)]
    up = lax.ppermute(keys_values, "seq", onward)
    down = lax.ppermute(keys_values, "seq", back)

    piece = strips * local_columns
    room = -(-piece // 16) * 16
    own_grad = jnp.pad(grad_out.reshape(piece, model_width), ((0, room - piece), (0, 0)))
    pieces, last_hops = gathered(own_grad, tensor_shift)
    slots = 8 * room

    slot = lax.iota(jnp.int32, slots)
    block, row = slot // room, slot % room
    owner = (spot_x + block // 2) % 4 * 2 + (spot_low + block % 2) % 2
    place = row // local_columns * columns + owner * local_columns + row % local_columns
    place = jnp.where(row < piece, place, -1)
    cell = lax.iota(jnp.int32, tokens)
    perm = (place[:, None] == cell[None, :]).astype(BF16)
    perm_back = (cell[:, None] == place[None, :]).astype(BF16)
    hot = (cell[:, None] % columns // TILE_W == lax.iota(jnp.int32, 128)[None, :]).astype(BF16)

    own_mask = lax.dynamic_slice_in_dim(block_mask, seq_place, 1, 1).reshape(-1, OFFSETS)
    bias = mask_bias(window, own_mask, seq_place, row_tiles)

    flat_q = queries.reshape(tokens, channels)
    flat = [v.reshape(2, tokens, channels) for v in (keys_values, up, down)]

    def whole(shape):
        return pl.BlockSpec(shape, lambda h: (0,) * len(shape))

    q_spec = pl.BlockSpec((tokens, HEAD_DIM), lambda h: (0, h))
    kv_spec = pl.BlockSpec((2, tokens, HEAD_DIM), lambda h: (0, 0, h))
    half = channels // 2
    pairs = heads * tokens * 3 * tokens
    probs, attended, turned = kernel(
        forward_kernel,
        [
            ((heads, 3, tokens, tokens), BF16),
            ((slots, channels), BF16),
            ((2, heads, HEAD_DIM // 2, slots), BF16),
        ],
        [flat_q, *flat, bias, hot, perm, core],
        [
            q_spec,
            kv_spec,
            kv_spec,
            kv_spec,
            pl.BlockSpec((1, 3, columns, 128), lambda h: (h, 0, 0, 0)),
            whole((tokens, 128)),
            whole((slots, tokens)),
            SCALAR,
        ],
        [
            pl.BlockSpec((1, 3, tokens, tokens), lambda h: (h, 0, 0, 0)),
            pl.BlockSpec((slots, HEAD_DIM), lambda h: (0, h)),
            pl.BlockSpec((2, 1, HEAD_DIM // 2, slots), lambda h: (0, h, 0, 0)),
        ],
        grid=(heads,),
        after=last_hops,
        flops=pairs * 1500,
        moved=8 << 20,
    )
    turned = turned.reshape(channels, slots)

    wide = model_width // 8
    step = lax.iota(jnp.int32, 8)
    chips = (spot_z + step // 2) % 4 * 2 + (spot_y + step % 2) % 2

    def weight_half(e, after):
        spec = pl.BlockSpec((1, half, wide), lambda i, o: (i, 0, 0))
        return pl.pallas_call(
            weight_kernel,
            grid_spec=pltpu.PrefetchScalarGridSpec(
                num_scalar_prefetch=1,
                grid=(4,),
                in_specs=[pl.BlockSpec((channels, slots), lambda i, o: (0, 0))]
                + [pl.BlockSpec((p.shape[0], wide), lambda i, o: (0, o[i])) for p in pieces]
                + [ANYWHERE],
                out_specs=[spec] * 2,
            ),
            out_shape=[jax.ShapeDtypeStruct((4, half, wide), BF16)] * 2,
            cost_estimate=pl.CostEstimate(
                flops=slots * model_width * channels * 2,
                transcendentals=0,
                bytes_accessed=6 << 20,
            ),
        )(chips[e::2].astype(jnp.int32), turned, *pieces, after)

    keep1, send1 = weight_half(1, attended)
    came1 = seq_shift(send1, 0, 0, 1)
    keep0, send0 = weight_half(0, send1)
    came0 = seq_shift(send0, 0, 0, 1)

    uppers = tops(room)
    shapes = [((n, model_width), BF16) for e in (1, 0) for n in part_rows(room, uppers[e])]
    broad = 2 * wide
    mixed_parts = kernel(
        project_kernel,
        shapes,
        [attended, out_weight],
        [whole((slots, channels)), pl.BlockSpec((channels, broad), lambda i: (0, i))],
        [pl.BlockSpec((n[0][0], broad), lambda i: (0, i)) for n in shapes],
        grid=(4,),
        after=[send0],
        flops=slots * model_width * channels * 3,
        moved=12 << 20,
    )
    mixed_parts = {1: mixed_parts[:5], 0: mixed_parts[5:]}
    mixed_came = {e: hop(tensor_shift, mixed_parts[e]) for e in (1, 0)}

    def fold(keep, came, after):
        return kernel(
            fold_kernel,
            [((n, wide), BF16) for n in part_rows(half, half // 2)],
            [keep, came],
            after=[after],
            flops=1 << 20,
            moved=5 << 20,
        )

    weight_parts = {1: fold(keep1, came1, mixed_parts[0][0])}
    weight_parts[0] = fold(keep0, came0, weight_parts[1][0])
    weight_came = {e: hop(seq_shift, weight_parts[e]) for e in (1, 0)}

    (grad_attn,) = kernel(
        attn_grad_kernel,
        [((slots, channels), BF16)],
        [out_weight, *pieces],
        [pl.BlockSpec((channels, broad), lambda i: (0, i))]
        + [pl.BlockSpec((p.shape[0], broad), lambda i: (0, i)) for p in pieces],
        [whole((slots, channels))],
        grid=(4,),
        after=[weight_parts[0][0]],
        flops=slots * model_width * channels * 3,
        moved=12 << 20,
        scratch=[pltpu.VMEM((slots, channels), F32)],
    )

    def differentiate(first, count, after):
        def spec(shape, at):
            def index(h):
                return tuple(h + first if i == at else 0 for i in range(len(shape)))

            return pl.BlockSpec(shape, index)

        width = count * HEAD_DIM
        kv_in = spec((2, tokens, HEAD_DIM), 2)
        return kernel(
            backward_kernel,
            [
                ((tokens, width), BF16),
                ((2, tokens, width), F32),
                ((2, tokens, width), BF16),
                ((2, tokens, width), BF16),
            ],
            [flat_q, *flat, probs, grad_attn, perm_back],
            [
                spec((tokens, HEAD_DIM), 1),
                kv_in,
                kv_in,
                kv_in,
                spec((1, 3, tokens, tokens), 0),
                spec((slots, HEAD_DIM), 1),
                whole((tokens, slots)),
            ],
            [q_spec, kv_spec, kv_spec, kv_spec],
            grid=(count,),
            after=after,
            flops=pairs * 2000 * count // heads,
            moved=2 * count << 20,
        )

    def send_halo(grad_up, grad_down):
        from_below = lax.ppermute(grad_up, "seq", back)
        from_above = lax.ppermute(grad_down, "seq", onward)
        return from_below, from_above

    def relay(parts, came, shift, after):
        sums = kernel(
            relay_kernel,
            [(parts[2].shape, BF16), (parts[3].shape, BF16)],
            [parts[2], parts[3], *came],
            after=after,
            moved=1 << 20,
        )
        return hop(shift, sums), sums[0]

    def side(parts, came, sums, shift, after):
        (total,) = kernel(
            side_kernel,
            [(parts[4].shape, BF16)],
            [parts[4], *came, *sums],
            after=after,
            moved=2 << 20,
        )
        return shift(total, 0, 1), total

    split = (heads + 1) // 2
    gq_a, own_a, up_a, down_a = differentiate(0, split, [])
    below_a, above_a = send_halo(up_a, down_a)
    mixed_sum1, mark = relay(mixed_parts[1], mixed_came[1], tensor_shift, [up_a])
    weight_sum1, mark = relay(weight_parts[1], weight_came[1], seq_shift, [mark])
    gq_b, own_b, up_b, down_b = differentiate(split, heads - split, [mark])
    below_b, above_b = send_halo(up_b, down_b)
    mixed_sum0, mark = relay(mixed_parts[0], mixed_came[0], tensor_shift, [up_b])
    weight_sum0, mark = relay(weight_parts[0], weight_came[0], seq_shift, [mark])
    mixed_side, mark = side(mixed_parts[1], mixed_came[1], mixed_sum1, tensor_shift, [mark])
    weight_side, mark = side(weight_parts[1], weight_came[1], weight_sum1, seq_shift, [mark])

    quarter = ((half, wide // 2), BF16)
    mine, other = kernel(
        split_kernel,
        [quarter, quarter],
        [weight_parts[0][4], *weight_came[0], *weight_sum0, weight_side, core],
        [VECTOR] * 6 + [SCALAR],
        after=[mark],
        moved=2 << 20,
    )
    other = seq_shift(other, 0, 0, 1)
    (layer_out,) = kernel(
        mixed_kernel,
        [((strips, local_columns, model_width), BF16)],
        [mixed_parts[0][4], *mixed_came[0], *mixed_sum0, mixed_side],
        after=[mine],
        moved=3 << 20,
    )
    (grad_weight,) = kernel(
        stack_kernel,
        [((channels, wide // 2), BF16)],
        [mine, other, core],
        [VECTOR] * 2 + [SCALAR],
        moved=1 << 20,
    )
    (grad_kv,) = kernel(
        total_kernel,
        [((2, tokens, channels), BF16)],
        [own_a, below_a, above_a, own_b, below_b, above_b],
        moved=5 << 20,
    )
    grad_q = jnp.concatenate([gq_a, gq_b], axis=1)
    return (
        layer_out.reshape(frames, tile_rows, local_columns, model_width),
        grad_q.reshape(queries.shape),
        grad_kv.reshape(keys_values.shape),
        grad_weight,
    )


def solution(mesh):
    return jax.shard_map(
        layer,
        mesh=mesh,
        in_specs=(
            P(None, "seq", None, "tensor"),
            P(None, None, "seq", None, "tensor"),
            P("tensor", None),
            P(None, "seq", "tensor", None),
            P("tensor", None),
            P(),
        ),
        out_specs=(
            P(None, "seq", "tensor", None),
            P(None, "seq", None, "tensor"),
            P(None, None, "seq", None, "tensor"),
            P("tensor", "seq"),
        ),
        check_vma=False,
    )
```

```python
import jax
import jax.numpy as jnp
import numpy as np
from jax import lax
from jax.experimental import pallas as pl
from jax.experimental.pallas import tpu as pltpu
from jax.sharding import PartitionSpec as P

HEAD_DIM = 128
TILE_W = 8
REACH_W = 3
OFFSETS = 63
SCALE = HEAD_DIM ** (-0.5)
OUTSIDE = -1e30
F32 = jnp.float32
BF16 = jnp.bfloat16


def dot(a, b, dims):
    return lax.dot_general(a, b, (dims, ((), ())), preferred_element_type=F32)


def tensor_shift(value, dx, dy):
    pairs = [
        (x * 2 + y, (x + dx) % 4 * 2 + (y + dy) % 2) for x in range(4) for y in range(2)
    ]
    return lax.ppermute(value, "tensor", pairs)


def seq_shift(value, dz, dy, core=0):
    pairs = [
        ((z * 2 + y) * 2 + c, ((z + dz) % 4 * 2 + (y + dy) % 2) * 2 + (c + core) % 2)
        for z in range(4)
        for y in range(2)
        for c in range(2)
    ]
    return lax.ppermute(value, "seq", pairs)


def added(*terms):
    total = terms[0].astype(F32)
    for term in terms[1:]:
        total = total + term.astype(F32)
    return total


BLOCKS = ((0, 0), (1, 0), (3, 0), (0, 1), (3, 1), (1, 1), (2, 0), (2, 1))


def gathered(own, shift):
    c01 = shift(own, 0, 1)
    c10 = shift(own, -1, 0)
    c30 = shift(own, 1, 0)
    c20 = shift(c10, -1, 0)
    c11 = shift(c01, -1, 0)
    c31 = shift(c01, 1, 0)
    c21 = shift(c31, 1, 0)
    return jnp.concatenate([own, c10, c30, c01, c31, c11, c20, c21], axis=0), [c10, c31]


ANYWHERE = pl.BlockSpec(memory_space=pl.ANY)


def kernel(body, outs, args, specs=None, out_specs=None, grid=(), after=(), flops=0, moved=0, scratch=()):
    count = len(args)

    def run(*refs):
        return body(*refs[:count], *refs[count + len(after) :])

    vector = pl.BlockSpec(memory_space=pltpu.VMEM)
    specs = [vector] * count if specs is None else specs
    out_specs = [vector] * len(outs) if out_specs is None else out_specs
    return pl.pallas_call(
        run,
        grid=grid,
        in_specs=[*specs, *[ANYWHERE] * len(after)],
        out_specs=out_specs,
        out_shape=[jax.ShapeDtypeStruct(shape, kind) for shape, kind in outs],
        scratch_shapes=scratch,
        cost_estimate=pl.CostEstimate(flops=flops, transcendentals=0, bytes_accessed=moved),
    )(*args, *after)


def sum_kernel(*refs):
    refs[-1][...] = added(*[r[...] for r in refs[:-1]]).astype(BF16)


def relay_kernel(a_ref, b_ref, came_a_ref, came_b_ref, out_a_ref, out_b_ref):
    out_a_ref[...] = added(a_ref[...], came_a_ref[...]).astype(BF16)
    out_b_ref[...] = added(b_ref[...], came_b_ref[...]).astype(BF16)


def mixed_kernel(*refs):
    out_ref = refs[-1]
    total = added(*[r[...] for r in refs[:-1]])
    frames, columns, rows, _ = out_ref.shape
    for f in range(frames):
        for c in range(columns):
            start = (f * columns + c) * rows
            out_ref[f, c] = total[start : start + rows].astype(BF16)


SCALAR = pl.BlockSpec(memory_space=pltpu.SMEM)
VECTOR = pl.BlockSpec(memory_space=pltpu.VMEM)


def hop(shift, arrays):
    return [shift(arrays[i], 1 - 2 * i, 0) for i in range(2)]


def forward_kernel(q_ref, own_ref, up_ref, down_ref, bias_ref, hot_ref, perm_ref, p_ref, att_ref):
    qa = jnp.concatenate([q_ref[...], hot_ref[...]], axis=1)
    scores = []
    for b, ref in enumerate((up_ref, own_ref, down_ref)):
        bias = jnp.concatenate([bias_ref[0, b]] * 9, axis=0).astype(BF16)
        ka = jnp.concatenate([ref[0], bias], axis=1)
        scores.append(dot(ka, qa, ((1,), (1,))))
    top = jnp.max(scores[0], axis=0, keepdims=True)
    for s in scores[1:]:
        top = jnp.maximum(top, jnp.max(s, axis=0, keepdims=True))
    weights = [jnp.exp((s - top) * SCALE) for s in scores]
    total = jnp.sum(weights[0], axis=0, keepdims=True)
    for w in weights[1:]:
        total = total + jnp.sum(w, axis=0, keepdims=True)
    inverse = 1.0 / total
    attended = None
    for b, ref in enumerate((up_ref, own_ref, down_ref)):
        probs = (weights[b] * inverse).astype(BF16)
        p_ref[0, b] = probs
        part = dot(ref[1], probs, ((0,), (0,)))
        attended = part if attended is None else attended + part
    attended = attended.astype(BF16)
    att_ref[...] = dot(perm_ref[...], attended, ((1,), (1,))).astype(BF16)


def backward_kernel(
    q_ref, own_ref, up_ref, down_ref, p_ref, ga_ref, perm_ref, gq_ref, gown_ref, gup_ref, gdown_ref
):
    q = q_ref[...]
    g = dot(perm_ref[...], ga_ref[...], ((1,), (0,))).astype(BF16)
    refs = (up_ref, own_ref, down_ref)
    outs = (gup_ref, gown_ref, gdown_ref)
    grads = []
    delta = None
    for b in range(3):
        gp = dot(refs[b][1], g, ((1,), (1,)))
        part = jnp.sum(p_ref[0, b].astype(F32) * gp, axis=0, keepdims=True)
        delta = part if delta is None else delta + part
        grads.append(gp)
    gq = None
    for b in range(3):
        probs = p_ref[0, b]
        ds = (probs.astype(F32) * (grads[b] - delta) * SCALE).astype(BF16)
        outs[b][0] = dot(ds, q, ((1,), (0,))).astype(outs[b].dtype)
        outs[b][1] = dot(probs, g, ((1,), (0,))).astype(outs[b].dtype)
        part = dot(refs[b][0], ds, ((0,), (0,)))
        gq = part if gq is None else gq + part
    gq_ref[...] = gq.T.astype(BF16)


def weight_kernel(order_ref, g_ref, far_g_ref, att_ref, far_att_ref, *outs):
    attended = jnp.concatenate([att_ref[...], far_att_ref[...]], axis=0)
    first = order_ref[len(outs)] == 0
    width = 2 * outs[0].shape[0]
    for i, out_ref in enumerate(outs):
        columns = pl.ds(pl.multiple_of(order_ref[i] * width, width), width)
        g = jnp.concatenate([g_ref[:, columns], far_g_ref[:, columns]], axis=0)
        g = jnp.where(first, g[:, : width // 2], g[:, width // 2 :])
        out_ref[...] = dot(g, attended, ((0,), (0,))).astype(BF16)


def project_kernel(att_ref, w_ref, *outs):
    mixed = dot(att_ref[...], w_ref[...], ((1,), (0,)))
    room = outs[0].shape[0]
    for k, out_ref in enumerate(outs):
        out_ref[...] = mixed[k * room : (k + 1) * room].astype(BF16)


def attn_grad_kernel(w_ref, g_ref, ga_ref, total_ref):
    step = pl.program_id(0)
    part = dot(g_ref[...], w_ref[...], ((1,), (1,)))

    @pl.when(step == 0)
    def _():
        total_ref[...] = part

    @pl.when(step > 0)
    def _():
        total_ref[...] += part

    @pl.when(step == pl.num_programs(0) - 1)
    def _():
        ga_ref[...] = total_ref[...].astype(BF16)


def total_kernel(*refs):
    out_ref = refs[-1]
    start = 0
    for i in range(0, len(refs) - 1, 3):
        part = added(refs[i][...], refs[i + 1][...], refs[i + 2][...]).astype(BF16)
        out_ref[:, :, start : start + part.shape[2]] = part
        start += part.shape[2]


def mask_bias(window, own_mask, seq_place, row_tiles):
    heads = window.shape[0]
    columns = own_mask.shape[0]
    rows = own_mask.reshape(columns, 3, 3, 7)[:, 1]
    query = np.arange(columns)
    delta = query[:, None] - query[None, :]
    pick = (delta[:, :, None] + REACH_W == np.arange(7)).astype(np.int32)
    bits = jnp.sum(rows.transpose(1, 0, 2)[:, None] * pick[None], axis=-1)
    dh = jnp.arange(3, dtype=jnp.int32) - 1
    tile_row = dh + seq_place
    row_ok = (tile_row >= 0) & (tile_row < row_tiles)
    inside = (jnp.abs(dh)[None, :] <= window[:, 1:2]) & row_ok[None, :] & (window[:, :1] >= 0)
    near = np.abs(delta)[None] <= window[:, 2][:, None, None]
    ok = inside[:, :, None, None] & near[:, None] & (bits > 0)[None]
    bias = jnp.where(ok, 0.0, OUTSIDE).astype(F32)
    bias = jnp.pad(bias, ((0, 0), (0, 0), (0, 0), (0, 128 - columns)))
    wide = jnp.broadcast_to(bias[:, :, :, None], (heads, 3, columns, TILE_W, 128))
    return wide.reshape(heads, 3, columns * TILE_W, 128)


def layer(queries, keys_values, out_weight, grad_out, window, block_mask):
    frames, tile_rows, columns, channels = queries.shape
    model_width = grad_out.shape[3]
    local_columns = grad_out.shape[2]
    tokens = frames * tile_rows * columns
    heads = channels // HEAD_DIM
    strips = frames * tile_rows
    row_tiles = lax.axis_size("seq")
    seq_place = lax.axis_index("seq")
    tensor_place = lax.axis_index("tensor")
    spot_z, spot_y, core = seq_place // 4, seq_place // 2 % 2, seq_place % 2
    spot_x, spot_low = tensor_place // 2, tensor_place % 2
    core = core[None].astype(jnp.int32)

    onward = [(i, i + 1) for i in range(row_tiles - 1)]
    back = [(i + 1, i) for i in range(row_tiles - 1)]
    up = lax.ppermute(keys_values, "seq", onward)
    down = lax.ppermute(keys_values, "seq", back)

    piece = strips * local_columns
    room = -(-piece // 16) * 16
    own_grad = grad_out.transpose(0, 2, 1, 3).reshape(piece, model_width)
    own_grad = jnp.pad(own_grad, ((0, room - piece), (0, 0)))
    all_grad, last_hops = gathered(own_grad, tensor_shift)
    slots = 8 * room

    row = np.arange(slots) % room
    ring, pair = (np.repeat([b[i] for b in BLOCKS], room).astype(np.int32) for i in range(2))
    owner = (spot_x + ring) % 4 * 2 + (spot_low + pair) % 2
    strip = row // (local_columns * tile_rows) * tile_rows + row % tile_rows
    place = strip * columns + owner * local_columns + row // tile_rows % local_columns
    place = jnp.where(row < piece, place, -1).astype(jnp.int32)
    cell = lax.iota(jnp.int32, tokens)
    perm = (place[:, None] == cell[None, :]).astype(BF16)
    perm_back = (cell[:, None] == place[None, :]).astype(BF16)
    hot = (cell[:, None] % columns // TILE_W == lax.iota(jnp.int32, 128)[None, :]).astype(BF16)

    own_mask = lax.dynamic_slice_in_dim(block_mask, seq_place, 1, 1).reshape(-1, OFFSETS)
    bias = mask_bias(window, own_mask, seq_place, row_tiles)

    flat_q = queries.reshape(tokens, channels)
    flat = [v.reshape(2, tokens, channels) for v in (keys_values, up, down)]

    def whole(shape):
        return pl.BlockSpec(shape, lambda h: (0,) * len(shape))

    q_spec = pl.BlockSpec((tokens, HEAD_DIM), lambda h: (0, h))
    kv_spec = pl.BlockSpec((2, tokens, HEAD_DIM), lambda h: (0, 0, h))
    pairs = heads * tokens * 3 * tokens
    probs, attended = kernel(
        forward_kernel,
        [((heads, 3, tokens, tokens), BF16), ((slots, channels), BF16)],
        [flat_q, *flat, bias, hot, perm],
        [
            q_spec,
            kv_spec,
            kv_spec,
            kv_spec,
            pl.BlockSpec((1, 3, columns, 128), lambda h: (h, 0, 0, 0)),
            whole((tokens, 128)),
            whole((slots, tokens)),
        ],
        [
            pl.BlockSpec((1, 3, tokens, tokens), lambda h: (h, 0, 0, 0)),
            pl.BlockSpec((slots, HEAD_DIM), lambda h: (0, h)),
        ],
        grid=(heads,),
        after=last_hops,
        flops=pairs * 1500,
        moved=8 << 20,
    )
    far_grad = seq_shift(all_grad, 0, 0, 1)
    far_attended = seq_shift(attended, 0, 0, 1)

    broad = model_width // 4
    mixed = kernel(
        project_kernel,
        [((room, model_width), BF16)] * 8,
        [attended, out_weight],
        [whole((slots, channels)), pl.BlockSpec((channels, broad), lambda i: (0, i))],
        [pl.BlockSpec((room, broad), lambda i: (0, i))] * 8,
        grid=(4,),
        flops=slots * model_width * channels * 3,
        moved=12 << 20,
    )
    mixed = dict(zip(BLOCKS, mixed))
    mixed_far = hop(tensor_shift, (mixed[2, 1], mixed[2, 0]))
    mixed_near = hop(tensor_shift, (mixed[1, 0], mixed[3, 1]))

    narrow = model_width // row_tiles

    def weight_blocks(blocks, after):
        chips = [(spot_z + d) % 4 * 2 + (spot_y + e) % 2 for d, e in blocks]
        order = jnp.stack([*chips, core[0]]).astype(jnp.int32)
        return kernel(
            weight_kernel,
            [((narrow, channels), BF16)] * len(blocks),
            [order, all_grad, far_grad, attended, far_attended],
            [SCALAR] + [VECTOR] * 4,
            after=after,
            flops=slots * model_width * channels * 2,
            moved=6 << 20,
        )

    w21, w20, w10, w31 = weight_blocks([(2, 1), (2, 0), (1, 0), (3, 1)], [mixed[0, 0]])
    weight_far = hop(seq_shift, (w21, w20))
    weight_near = hop(seq_shift, (w10, w31))
    w11, w30, w01, w00 = weight_blocks([(1, 1), (3, 0), (0, 1), (0, 0)], [w21])

    (grad_attn,) = kernel(
        attn_grad_kernel,
        [((slots, channels), BF16)],
        [out_weight, all_grad],
        [
            pl.BlockSpec((channels, broad), lambda i: (0, i)),
            pl.BlockSpec((slots, broad), lambda i: (0, i)),
        ],
        [whole((slots, channels))],
        grid=(4,),
        after=[w11],
        flops=slots * model_width * channels * 3,
        moved=12 << 20,
        scratch=[pltpu.VMEM((slots, channels), F32)],
    )

    def differentiate(first, count, after):
        def spec(shape, at):
            def index(h):
                return tuple(h + first if i == at else 0 for i in range(len(shape)))

            return pl.BlockSpec(shape, index)

        width = count * HEAD_DIM
        kv_in = spec((2, tokens, HEAD_DIM), 2)
        return kernel(
            backward_kernel,
            [
                ((tokens, width), BF16),
                ((2, tokens, width), F32),
                ((2, tokens, width), BF16),
                ((2, tokens, width), BF16),
            ],
            [flat_q, *flat, probs, grad_attn, perm_back],
            [
                spec((tokens, HEAD_DIM), 1),
                kv_in,
                kv_in,
                kv_in,
                spec((1, 3, tokens, tokens), 0),
                spec((slots, HEAD_DIM), 1),
                whole((tokens, slots)),
            ],
            [q_spec, kv_spec, kv_spec, kv_spec],
            grid=(count,),
            after=after,
            flops=pairs * 2000 * count // heads,
            moved=2 * count << 20,
        )

    def send_halo(grad_up, grad_down):
        from_below = lax.ppermute(grad_up, "seq", back)
        from_above = lax.ppermute(grad_down, "seq", onward)
        return from_below, from_above

    def summed(body, shapes, terms, after):
        return kernel(body, [(shape, BF16) for shape in shapes], terms, after=after, moved=2 << 20)

    split = (heads + 1) // 2
    mixed_sums = summed(
        relay_kernel, [own_grad.shape] * 2, [mixed[1, 1], mixed[3, 0], *mixed_far], [grad_attn]
    )
    mark = mixed_sums[0]
    mixed_sums = hop(tensor_shift, mixed_sums)
    gq_a, own_a, up_a, down_a = differentiate(0, split, [mark])
    below_a, above_a = send_halo(up_a, down_a)
    weight_sums = summed(relay_kernel, [w00.shape] * 2, [w11, w30, *weight_far], [up_a])
    mark = weight_sums[0]
    weight_sums = hop(seq_shift, weight_sums)
    gq_b, own_b, up_b, down_b = differentiate(split, heads - split, [mark])
    below_b, above_b = send_halo(up_b, down_b)
    (side,) = summed(
        sum_kernel, [own_grad.shape], [mixed[0, 1], mixed_near[1], mixed_sums[0]], [up_b]
    )
    mixed_side = tensor_shift(side, 0, 1)
    (side,) = summed(sum_kernel, [w00.shape], [w01, weight_near[1], weight_sums[0]], [side])
    weight_side = seq_shift(side, 0, 1)
    (grad_kv,) = summed(
        total_kernel,
        [(2, tokens, channels)],
        [own_a, below_a, above_a, own_b, below_b, above_b],
        [side],
    )
    (layer_out,) = summed(
        mixed_kernel,
        [(frames, local_columns, tile_rows, model_width)],
        [mixed[0, 0], mixed_near[0], mixed_sums[1], mixed_side],
        [grad_kv],
    )
    (grad_weight,) = summed(
        sum_kernel, [w00.shape], [w00, weight_near[0], weight_sums[1], weight_side], [layer_out]
    )
    grad_q = jnp.concatenate([gq_a, gq_b], axis=1)
    return (
        layer_out.transpose(0, 2, 1, 3),
        grad_q.reshape(queries.shape),
        grad_kv.reshape(keys_values.shape),
        grad_weight.T,
    )


def solution(mesh):
    return jax.shard_map(
        layer,
        mesh=mesh,
        in_specs=(
            P(None, "seq", None, "tensor"),
            P(None, None, "seq", None, "tensor"),
            P("tensor", None),
            P(None, "seq", "tensor", None),
            P("tensor", None),
            P(),
        ),
        out_specs=(
            P(None, "seq", "tensor", None),
            P(None, "seq", None, "tensor"),
            P(None, None, "seq", None, "tensor"),
            P("tensor", "seq"),
        ),
        check_vma=False,
    )
```

```python
import jax
import jax.numpy as jnp
import numpy as np
from jax import lax
from jax.experimental import pallas as pl
from jax.experimental.pallas import tpu as pltpu
from jax.sharding import PartitionSpec as P

HEAD_DIM = 128
TILE_W = 8
REACH_W = 3
OFFSETS = 63
SCALE = HEAD_DIM ** (-0.5)
OUTSIDE = -1e30
F32 = jnp.float32
BF16 = jnp.bfloat16


def dot(a, b, dims):
    return lax.dot_general(a, b, (dims, ((), ())), preferred_element_type=F32)


def tensor_shift(value, dx, dy):
    pairs = [
        (x * 2 + y, (x + dx) % 4 * 2 + (y + dy) % 2) for x in range(4) for y in range(2)
    ]
    return lax.ppermute(value, "tensor", pairs)


def seq_shift(value, dz, dy, core=0):
    pairs = [
        ((z * 2 + y) * 2 + c, ((z + dz) % 4 * 2 + (y + dy) % 2) * 2 + (c + core) % 2)
        for z in range(4)
        for y in range(2)
        for c in range(2)
    ]
    return lax.ppermute(value, "seq", pairs)


def added(*terms):
    total = terms[0].astype(F32)
    for term in terms[1:]:
        total = total + term.astype(F32)
    return total


BLOCKS = ((0, 0), (1, 0), (3, 0), (0, 1), (3, 1), (1, 1), (2, 0), (2, 1))


def gathered(own, shift):
    c01 = shift(own, 0, 1)
    c10 = shift(own, -1, 0)
    c30 = shift(own, 1, 0)
    c20 = shift(c10, -1, 0)
    c11 = shift(c01, -1, 0)
    c31 = shift(c01, 1, 0)
    c21 = shift(c31, 1, 0)
    return jnp.concatenate([own, c10, c30, c01, c31, c11, c20, c21], axis=0), [c10, c31]


ROOM = 24 << 20
ANYWHERE = pl.BlockSpec(memory_space=pl.ANY)


def kernel(body, outs, args, specs=None, out_specs=None, grid=(), after=(), flops=0, moved=0, scratch=()):
    count = len(args)

    def run(*refs):
        return body(*refs[:count], *refs[count + len(after) :])

    vector = pl.BlockSpec(memory_space=pltpu.VMEM)
    specs = [vector] * count if specs is None else specs
    out_specs = [vector] * len(outs) if out_specs is None else out_specs
    return pl.pallas_call(
        run,
        grid=grid,
        in_specs=[*specs, *[ANYWHERE] * len(after)],
        out_specs=out_specs,
        out_shape=[jax.ShapeDtypeStruct(shape, kind) for shape, kind in outs],
        scratch_shapes=scratch,
        compiler_params=pltpu.CompilerParams(vmem_limit_bytes=ROOM),
        cost_estimate=pl.CostEstimate(flops=flops, transcendentals=0, bytes_accessed=moved),
    )(*args, *after)


def mixed_kernel(*refs):
    out_ref = refs[-1]
    total = added(*[r[...] for r in refs[:-1]])
    frames, columns, rows, _ = out_ref.shape
    for f in range(frames):
        for c in range(columns):
            start = (f * columns + c) * rows
            out_ref[f, c] = total[start : start + rows].astype(BF16)


SCALAR = pl.BlockSpec(memory_space=pltpu.SMEM)
VECTOR = pl.BlockSpec(memory_space=pltpu.VMEM)


def hop(shift, arrays):
    return [shift(arrays[i], 1 - 2 * i, 0) for i in range(2)]


def forward_kernel(q_ref, own_ref, up_ref, down_ref, bias_ref, hot_ref, perm_ref, p_ref, att_ref):
    qa = jnp.concatenate([q_ref[...], hot_ref[...]], axis=1)
    scores = []
    for b, ref in enumerate((up_ref, own_ref, down_ref)):
        bias = jnp.concatenate([bias_ref[0, b]] * 9, axis=0).astype(BF16)
        ka = jnp.concatenate([ref[0], bias], axis=1)
        scores.append(dot(ka, qa, ((1,), (1,))))
    top = jnp.max(scores[0], axis=0, keepdims=True)
    for s in scores[1:]:
        top = jnp.maximum(top, jnp.max(s, axis=0, keepdims=True))
    weights = [jnp.exp((s - top) * SCALE) for s in scores]
    total = jnp.sum(weights[0], axis=0, keepdims=True)
    for w in weights[1:]:
        total = total + jnp.sum(w, axis=0, keepdims=True)
    inverse = 1.0 / total
    attended = None
    for b, ref in enumerate((up_ref, own_ref, down_ref)):
        probs = (weights[b] * inverse).astype(BF16)
        p_ref[0, b] = probs
        part = dot(ref[1], probs, ((0,), (0,)))
        attended = part if attended is None else attended + part
    attended = attended.astype(BF16)
    att_ref[...] = dot(perm_ref[...], attended, ((1,), (1,))).astype(BF16)


def backward_kernel(
    q_ref, own_ref, up_ref, down_ref, p_ref, ga_ref, perm_ref, gq_ref, gown_ref, gup_ref, gdown_ref
):
    q = q_ref[...]
    g = dot(perm_ref[...], ga_ref[...], ((1,), (0,))).astype(BF16)
    refs = (up_ref, own_ref, down_ref)
    outs = (gup_ref, gown_ref, gdown_ref)
    grads = []
    delta = None
    for b in range(3):
        gp = dot(refs[b][1], g, ((1,), (1,)))
        part = jnp.sum(p_ref[0, b].astype(F32) * gp, axis=0, keepdims=True)
        delta = part if delta is None else delta + part
        grads.append(gp)
    gq = None
    for b in range(3):
        probs = p_ref[0, b]
        ds = (probs.astype(F32) * (grads[b] - delta) * SCALE).astype(BF16)
        outs[b][0] = dot(ds, q, ((1,), (0,))).astype(outs[b].dtype)
        outs[b][1] = dot(probs, g, ((1,), (0,))).astype(outs[b].dtype)
        part = dot(refs[b][0], ds, ((0,), (0,)))
        gq = part if gq is None else gq + part
    gq_ref[...] = gq.T.astype(BF16)


def weight_kernel(order_ref, *refs):
    parts, (att_ref, far_att_ref), outs = refs[:6], refs[6:8], refs[8:]
    attended = jnp.concatenate([att_ref[...], far_att_ref[...]], axis=0)
    turned = [jnp.concatenate([p[...].T for p in parts[3 * i : 3 * i + 3]], axis=0) for i in range(2)]
    turned = jnp.concatenate(turned, axis=1)
    rows = outs[0].shape[0]
    extra = turned.shape[0] - rows
    turned = jnp.where(order_ref[len(outs)] == 0, turned[:rows], turned[extra:])
    grad = dot(turned, attended, ((1,), (0,))).astype(BF16)
    step = pl.program_id(0)
    for i, out_ref in enumerate(outs):

        @pl.when(step == i)
        def _(out_ref=out_ref):
            out_ref[...] = grad


def project_kernel(att_ref, w_ref, *outs):
    mixed = dot(att_ref[...], w_ref[...], ((1,), (0,)))
    room = outs[0].shape[0]
    for k, out_ref in enumerate(outs):
        out_ref[...] = mixed[k * room : (k + 1) * room].astype(BF16)


def attn_grad_kernel(w_ref, g_ref, ga_ref, total_ref):
    step = pl.program_id(0)
    part = dot(g_ref[...], w_ref[...], ((1,), (1,)))

    @pl.when(step == 0)
    def _():
        total_ref[...] = part

    @pl.when(step > 0)
    def _():
        total_ref[...] += part

    @pl.when(step == pl.num_programs(0) - 1)
    def _():
        ga_ref[...] = total_ref[...].astype(BF16)


def mask_bias(window, own_mask, seq_place, row_tiles):
    heads = window.shape[0]
    columns = own_mask.shape[0]
    rows = own_mask.reshape(columns, 3, 3, 7)[:, 1]
    query = np.arange(columns)
    delta = query[:, None] - query[None, :]
    pick = (delta[:, :, None] + REACH_W == np.arange(7)).astype(np.int32)
    bits = jnp.sum(rows.transpose(1, 0, 2)[:, None] * pick[None], axis=-1)
    dh = jnp.arange(3, dtype=jnp.int32) - 1
    tile_row = dh + seq_place
    row_ok = (tile_row >= 0) & (tile_row < row_tiles)
    inside = (jnp.abs(dh)[None, :] <= window[:, 1:2]) & row_ok[None, :] & (window[:, :1] >= 0)
    near = np.abs(delta)[None] <= window[:, 2][:, None, None]
    ok = inside[:, :, None, None] & near[:, None] & (bits > 0)[None]
    bias = jnp.where(ok, 0.0, OUTSIDE).astype(F32)
    bias = jnp.pad(bias, ((0, 0), (0, 0), (0, 0), (0, 128 - columns)))
    wide = jnp.broadcast_to(bias[:, :, :, None], (heads, 3, columns, TILE_W, 128))
    return wide.reshape(heads, 3, columns * TILE_W, 128)


def layer(queries, keys_values, out_weight, grad_out, window, block_mask):
    frames, tile_rows, columns, channels = queries.shape
    model_width = grad_out.shape[3]
    local_columns = grad_out.shape[2]
    tokens = frames * tile_rows * columns
    heads = channels // HEAD_DIM
    strips = frames * tile_rows
    row_tiles = lax.axis_size("seq")
    seq_place = lax.axis_index("seq")
    tensor_place = lax.axis_index("tensor")
    spot_z, spot_y, core = seq_place // 4, seq_place // 2 % 2, seq_place % 2
    spot_x, spot_low = tensor_place // 2, tensor_place % 2
    core = core[None].astype(jnp.int32)

    onward = [(i, i + 1) for i in range(row_tiles - 1)]
    back = [(i + 1, i) for i in range(row_tiles - 1)]
    up = lax.ppermute(keys_values, "seq", onward)
    down = lax.ppermute(keys_values, "seq", back)

    piece = strips * local_columns
    room = -(-piece // 16) * 16
    own_grad = grad_out.transpose(0, 2, 1, 3).reshape(piece, model_width)
    own_grad = jnp.pad(own_grad, ((0, room - piece), (0, 0)))
    all_grad, last_hops = gathered(own_grad, tensor_shift)
    slots = 8 * room

    row = np.arange(slots) % room
    ring, pair = (np.repeat([b[i] for b in BLOCKS], room).astype(np.int32) for i in range(2))
    owner = (spot_x + ring) % 4 * 2 + (spot_low + pair) % 2
    strip = row // (local_columns * tile_rows) * tile_rows + row % tile_rows
    place = strip * columns + owner * local_columns + row // tile_rows % local_columns
    place = jnp.where(row < piece, place, -1).astype(jnp.int32)
    cell = lax.iota(jnp.int32, tokens)
    perm = (place[:, None] == cell[None, :]).astype(BF16)
    perm_back = (cell[:, None] == place[None, :]).astype(BF16)
    hot = (cell[:, None] % columns // TILE_W == lax.iota(jnp.int32, 128)[None, :]).astype(BF16)

    own_mask = lax.dynamic_slice_in_dim(block_mask, seq_place, 1, 1).reshape(-1, OFFSETS)
    bias = mask_bias(window, own_mask, seq_place, row_tiles)

    flat_q = queries.reshape(tokens, channels)
    flat = [v.reshape(2, tokens, channels) for v in (keys_values, up, down)]

    def whole(shape):
        return pl.BlockSpec(shape, lambda h: (0,) * len(shape))

    q_spec = pl.BlockSpec((tokens, HEAD_DIM), lambda h: (0, h))
    kv_spec = pl.BlockSpec((2, tokens, HEAD_DIM), lambda h: (0, 0, h))
    weights = ((2, 1), (2, 0), (1, 0), (3, 1), (1, 1), (3, 0), (0, 1), (0, 0))
    ring, pair = (np.array([w[i] for w in weights], np.int32) for i in range(2))
    chips = (spot_z + ring) % 4 * 2 + (spot_y + pair) % 2
    order = jnp.concatenate([chips, core]).astype(jnp.int32)

    pairs = heads * tokens * 3 * tokens
    probs, attended = kernel(
        forward_kernel,
        [((heads, 3, tokens, tokens), BF16), ((slots, channels), BF16)],
        [flat_q, *flat, bias, hot, perm],
        [
            q_spec,
            kv_spec,
            kv_spec,
            kv_spec,
            pl.BlockSpec((1, 3, columns, 128), lambda h: (h, 0, 0, 0)),
            whole((tokens, 128)),
            whole((slots, tokens)),
        ],
        [
            pl.BlockSpec((1, 3, tokens, tokens), lambda h: (h, 0, 0, 0)),
            pl.BlockSpec((slots, HEAD_DIM), lambda h: (0, h)),
        ],
        grid=(heads,),
        after=[*last_hops, perm_back, order],
        flops=pairs * 1500,
        moved=8 << 20,
    )
    far_grad = seq_shift(all_grad, 0, 0, 1)
    far_attended = seq_shift(attended, 0, 0, 1)

    broad = model_width // 4
    mixed = kernel(
        project_kernel,
        [((room, model_width), BF16)] * 8,
        [attended, out_weight],
        [whole((slots, channels)), pl.BlockSpec((channels, broad), lambda i: (0, i))],
        [pl.BlockSpec((room, broad), lambda i: (0, i))] * 8,
        grid=(4,),
        flops=slots * model_width * channels * 3,
        moved=12 << 20,
    )
    mixed = dict(zip(BLOCKS, mixed))
    mixed_far = hop(tensor_shift, (mixed[2, 1], mixed[2, 0]))
    mixed_near = hop(tensor_shift, (mixed[1, 0], mixed[3, 1]))

    narrow = model_width // row_tiles
    lanes = 128
    window_specs = [
        pl.BlockSpec((slots, lanes), lambda i, o, j=j: (0, o[i] * (2 * narrow // lanes) + 2 * o[8] + j))
        for j in range(3)
    ]

    def constant(shape):
        return pl.BlockSpec(shape, lambda i, o: (0, 0))

    weight = pl.pallas_call(
        weight_kernel,
        grid_spec=pltpu.PrefetchScalarGridSpec(
            num_scalar_prefetch=1,
            grid=(8,),
            in_specs=[*window_specs, *window_specs, *[constant((slots, channels))] * 2],
            out_specs=[constant((narrow, channels))] * 8,
        ),
        out_shape=[jax.ShapeDtypeStruct((narrow, channels), BF16)] * 8,
        compiler_params=pltpu.CompilerParams(vmem_limit_bytes=ROOM),
        cost_estimate=pl.CostEstimate(
            flops=slots * model_width * channels * 2, transcendentals=0, bytes_accessed=9 << 20
        ),
    )(order, *[all_grad] * 3, *[far_grad] * 3, attended, far_attended)
    weight = dict(zip(weights, weight))
    weight_far = hop(seq_shift, (weight[2, 1], weight[2, 0]))
    weight_near = hop(seq_shift, (weight[1, 0], weight[3, 1]))

    (grad_attn,) = kernel(
        attn_grad_kernel,
        [((slots, channels), BF16)],
        [out_weight, all_grad],
        [
            pl.BlockSpec((channels, broad), lambda i: (0, i)),
            pl.BlockSpec((slots, broad), lambda i: (0, i)),
        ],
        [whole((slots, channels))],
        grid=(4,),
        after=[weight[0, 0]],
        flops=slots * model_width * channels * 3,
        moved=12 << 20,
        scratch=[pltpu.VMEM((slots, channels), F32)],
    )

    wide = ((2, tokens, channels), BF16)
    grad_q, grad_own, grad_up, grad_down = kernel(
        backward_kernel,
        [((tokens, channels), BF16), (wide[0], F32), wide, wide],
        [flat_q, *flat, probs, grad_attn, perm_back],
        [
            q_spec,
            kv_spec,
            kv_spec,
            kv_spec,
            pl.BlockSpec((1, 3, tokens, tokens), lambda h: (h, 0, 0, 0)),
            pl.BlockSpec((slots, HEAD_DIM), lambda h: (0, h)),
            whole((tokens, slots)),
        ],
        [q_spec, kv_spec, kv_spec, kv_spec],
        grid=(heads,),
        flops=pairs * 2000,
        moved=12 << 20,
    )

    def relayed(kept, came, shift):
        sums = [added(k, c).astype(BF16) for k, c in zip(kept, came)]
        return hop(shift, sums)

    def side(shift, *terms):
        total = added(*terms).astype(BF16)
        return shift(total, 0, 1)

    mixed_sums = relayed((mixed[1, 1], mixed[3, 0]), mixed_far, tensor_shift)
    weight_sums = relayed((weight[1, 1], weight[3, 0]), weight_far, seq_shift)
    mixed_side = side(tensor_shift, mixed[0, 1], mixed_near[1], mixed_sums[0])
    weight_side = side(seq_shift, weight[0, 1], weight_near[1], weight_sums[0])
    from_below = lax.ppermute(grad_up, "seq", back)
    from_above = lax.ppermute(grad_down, "seq", onward)

    (layer_out,) = kernel(
        mixed_kernel,
        [((frames, local_columns, tile_rows, model_width), BF16)],
        [mixed[0, 0], mixed_near[0], mixed_sums[1], mixed_side],
        moved=3 << 20,
    )
    grad_weight = added(weight[0, 0], weight_near[0], weight_sums[1], weight_side).astype(BF16)
    grad_kv = added(grad_own, from_below, from_above).astype(BF16)
    return (
        layer_out.transpose(0, 2, 1, 3),
        grad_q.reshape(queries.shape),
        grad_kv.reshape(keys_values.shape),
        grad_weight.T,
    )


def solution(mesh):
    return jax.shard_map(
        layer,
        mesh=mesh,
        in_specs=(
            P(None, "seq", None, "tensor"),
            P(None, None, "seq", None, "tensor"),
            P("tensor", None),
            P(None, "seq", "tensor", None),
            P("tensor", None),
            P(),
        ),
        out_specs=(
            P(None, "seq", "tensor", None),
            P(None, "seq", None, "tensor"),
            P(None, None, "seq", None, "tensor"),
            P("tensor", "seq"),
        ),
        check_vma=False,
    )
```

```python
import jax
import jax.numpy as jnp
import numpy as np
from jax import lax
from jax.experimental import pallas as pl
from jax.experimental.pallas import tpu as pltpu
from jax.sharding import PartitionSpec as P

HEAD_DIM = 128
TILE_W = 8
REACH_W = 3
OFFSETS = 63
SCALE = HEAD_DIM ** (-0.5)
OUTSIDE = -1e30
F32 = jnp.float32
BF16 = jnp.bfloat16


def dot(a, b, dims):
    return lax.dot_general(a, b, (dims, ((), ())), preferred_element_type=F32)


def tensor_shift(value, dx, dy):
    pairs = [
        (x * 2 + y, (x + dx) % 4 * 2 + (y + dy) % 2) for x in range(4) for y in range(2)
    ]
    return lax.ppermute(value, "tensor", pairs)


def seq_shift(value, dz, dy, core=0):
    pairs = [
        ((z * 2 + y) * 2 + c, ((z + dz) % 4 * 2 + (y + dy) % 2) * 2 + (c + core) % 2)
        for z in range(4)
        for y in range(2)
        for c in range(2)
    ]
    return lax.ppermute(value, "seq", pairs)


def added(*terms):
    total = terms[0].astype(F32)
    for term in terms[1:]:
        total = total + term.astype(F32)
    return total


BLOCKS = ((0, 0), (1, 0), (3, 0), (0, 1), (3, 1), (1, 1), (2, 0), (2, 1))


def gathered(own, shift):
    c01 = shift(own, 0, 1)
    c10 = shift(own, -1, 0)
    c30 = shift(own, 1, 0)
    c20 = shift(c10, -1, 0)
    c11 = shift(c01, -1, 0)
    c31 = shift(c01, 1, 0)
    c21 = shift(c31, 1, 0)
    return jnp.concatenate([own, c10, c30, c01, c31, c11, c20, c21], axis=0), [c10, c31]


ROOM = 24 << 20
ANYWHERE = pl.BlockSpec(memory_space=pl.ANY)


def kernel(body, outs, args, specs=None, out_specs=None, grid=(), after=(), flops=0, moved=0, scratch=()):
    count = len(args)

    def run(*refs):
        return body(*refs[:count], *refs[count + len(after) :])

    vector = pl.BlockSpec(memory_space=pltpu.VMEM)
    specs = [vector] * count if specs is None else specs
    out_specs = [vector] * len(outs) if out_specs is None else out_specs
    return pl.pallas_call(
        run,
        grid=grid,
        in_specs=[*specs, *[ANYWHERE] * len(after)],
        out_specs=out_specs,
        out_shape=[jax.ShapeDtypeStruct(shape, kind) for shape, kind in outs],
        scratch_shapes=scratch,
        compiler_params=pltpu.CompilerParams(vmem_limit_bytes=ROOM),
        cost_estimate=pl.CostEstimate(flops=flops, transcendentals=0, bytes_accessed=moved),
    )(*args, *after)


def mixed_kernel(*refs):
    out_ref = refs[-1]
    total = added(*[r[...] for r in refs[:-1]])
    frames, columns, rows, _ = out_ref.shape
    for f in range(frames):
        for c in range(columns):
            start = (f * columns + c) * rows
            out_ref[f, c] = total[start : start + rows].astype(BF16)


SCALAR = pl.BlockSpec(memory_space=pltpu.SMEM)
VECTOR = pl.BlockSpec(memory_space=pltpu.VMEM)


def hop(shift, arrays):
    return [shift(arrays[i], 1 - 2 * i, 0) for i in range(2)]


def scores_kernel(q_ref, own_ref, up_ref, down_ref, bias_ref, hot_ref, p_ref):
    qa = jnp.concatenate([q_ref[...], hot_ref[...]], axis=1)
    scores = []
    for b, ref in enumerate((up_ref, own_ref, down_ref)):
        bias = jnp.concatenate([bias_ref[0, b]] * 9, axis=0).astype(BF16)
        ka = jnp.concatenate([ref[...], bias], axis=1)
        scores.append(dot(ka, qa, ((1,), (1,))))
    top = jnp.max(scores[0], axis=0, keepdims=True)
    for s in scores[1:]:
        top = jnp.maximum(top, jnp.max(s, axis=0, keepdims=True))
    weights = [jnp.exp((s - top) * SCALE) for s in scores]
    total = jnp.sum(weights[0], axis=0, keepdims=True)
    for w in weights[1:]:
        total = total + jnp.sum(w, axis=0, keepdims=True)
    inverse = 1.0 / total
    for b in range(3):
        p_ref[0, b] = (weights[b] * inverse).astype(BF16)


def attend_kernel(p_ref, own_ref, up_ref, down_ref, perm_ref, att_ref):
    attended = None
    for b, ref in enumerate((up_ref, own_ref, down_ref)):
        part = dot(ref[...], p_ref[0, b], ((0,), (0,)))
        attended = part if attended is None else attended + part
    att_ref[...] = dot(perm_ref[...], attended.astype(BF16), ((1,), (1,))).astype(BF16)


def backward_kernel(q_ref, *refs):
    keys, values = (refs[1], refs[0], refs[2]), (refs[4], refs[3], refs[5])
    p_ref, ga_ref, perm_ref, gq_ref, gown_ref, gup_ref, gdown_ref = refs[6:]
    q = q_ref[...]
    g = dot(perm_ref[...], ga_ref[...], ((1,), (0,))).astype(BF16)
    outs = (gup_ref, gown_ref, gdown_ref)
    grads = []
    delta = None
    for b in range(3):
        gp = dot(values[b][...], g, ((1,), (1,)))
        part = jnp.sum(p_ref[0, b].astype(F32) * gp, axis=0, keepdims=True)
        delta = part if delta is None else delta + part
        grads.append(gp)
    gq = None
    for b in range(3):
        probs = p_ref[0, b]
        ds = (probs.astype(F32) * (grads[b] - delta) * SCALE).astype(BF16)
        outs[b][0] = dot(ds, q, ((1,), (0,))).astype(outs[b].dtype)
        outs[b][1] = dot(probs, g, ((1,), (0,))).astype(outs[b].dtype)
        part = dot(keys[b][...], ds, ((0,), (0,)))
        gq = part if gq is None else gq + part
    gq_ref[...] = gq.T.astype(BF16)


def total_kernel(*refs):
    out_ref = refs[-1]
    start = 0
    for i in range(0, len(refs) - 1, 3):
        part = added(refs[i][...], refs[i + 1][...], refs[i + 2][...]).astype(BF16)
        out_ref[:, :, start : start + part.shape[2]] = part
        start += part.shape[2]


def weight_kernel(order_ref, g_ref, far_g_ref, att_ref, far_att_ref, *outs):
    attended = jnp.concatenate([att_ref[...], far_att_ref[...]], axis=0)
    core = order_ref[len(outs)]
    rows = outs[0].shape[0]
    lanes = 128
    wide = -(-rows // lanes) * lanes
    for i, out_ref in enumerate(outs):
        start = order_ref[i] * (2 * rows) + core * (2 * rows - wide)
        columns = pl.ds(pl.multiple_of(start, lanes), wide)
        turned = jnp.concatenate([g_ref[:, columns].T, far_g_ref[:, columns].T], axis=1)
        turned = jnp.where(core == 0, turned[:rows], turned[wide - rows :])
        out_ref[...] = dot(turned, attended, ((1,), (0,))).astype(BF16)


def project_kernel(att_ref, w_ref, *outs):
    mixed = dot(att_ref[...], w_ref[...], ((1,), (0,)))
    room = outs[0].shape[0]
    for k, out_ref in enumerate(outs):
        out_ref[...] = mixed[k * room : (k + 1) * room].astype(BF16)


def attn_grad_kernel(w_ref, g_ref, ga_ref, total_ref):
    step = pl.program_id(0)
    part = dot(g_ref[...], w_ref[...], ((1,), (1,)))

    @pl.when(step == 0)
    def _():
        total_ref[...] = part

    @pl.when(step > 0)
    def _():
        total_ref[...] += part

    @pl.when(step == pl.num_programs(0) - 1)
    def _():
        ga_ref[...] = total_ref[...].astype(BF16)


def mask_bias(window, own_mask, seq_place, row_tiles):
    heads = window.shape[0]
    columns = own_mask.shape[0]
    rows = own_mask.reshape(columns, 3, 3, 7)[:, 1]
    query = np.arange(columns)
    delta = query[:, None] - query[None, :]
    pick = (delta[:, :, None] + REACH_W == np.arange(7)).astype(np.int32)
    bits = jnp.sum(rows.transpose(1, 0, 2)[:, None] * pick[None], axis=-1)
    dh = jnp.arange(3, dtype=jnp.int32) - 1
    tile_row = dh + seq_place
    row_ok = (tile_row >= 0) & (tile_row < row_tiles)
    inside = (jnp.abs(dh)[None, :] <= window[:, 1:2]) & row_ok[None, :] & (window[:, :1] >= 0)
    near = np.abs(delta)[None] <= window[:, 2][:, None, None]
    ok = inside[:, :, None, None] & near[:, None] & (bits > 0)[None]
    bias = jnp.where(ok, 0.0, OUTSIDE).astype(F32)
    bias = jnp.pad(bias, ((0, 0), (0, 0), (0, 0), (0, 128 - columns)))
    wide = jnp.broadcast_to(bias[:, :, :, None], (heads, 3, columns, TILE_W, 128))
    return wide.reshape(heads, 3, columns * TILE_W, 128)


def layer(queries, keys_values, out_weight, grad_out, window, block_mask):
    frames, tile_rows, columns, channels = queries.shape
    model_width = grad_out.shape[3]
    local_columns = grad_out.shape[2]
    tokens = frames * tile_rows * columns
    heads = channels // HEAD_DIM
    strips = frames * tile_rows
    row_tiles = lax.axis_size("seq")
    seq_place = lax.axis_index("seq")
    tensor_place = lax.axis_index("tensor")
    spot_z, spot_y, core = seq_place // 4, seq_place // 2 % 2, seq_place % 2
    spot_x, spot_low = tensor_place // 2, tensor_place % 2
    core = core[None].astype(jnp.int32)

    onward = [(i, i + 1) for i in range(row_tiles - 1)]
    back = [(i + 1, i) for i in range(row_tiles - 1)]
    flat_q = queries.reshape(tokens, channels)
    flat_kv = keys_values.reshape(2, tokens, channels)
    halos = []
    for i in range(2):
        up = lax.ppermute(flat_kv[i], "seq", onward)
        down = lax.ppermute(flat_kv[i], "seq", back)
        halos.append([flat_kv, up, down])

    piece = strips * local_columns
    room = -(-piece // 16) * 16
    own_grad = grad_out.transpose(0, 2, 1, 3).reshape(piece, model_width)
    own_grad = jnp.pad(own_grad, ((0, room - piece), (0, 0)))
    all_grad, last_hops = gathered(own_grad, tensor_shift)
    slots = 8 * room

    row = np.arange(slots) % room
    ring, pair = (np.repeat([b[i] for b in BLOCKS], room).astype(np.int32) for i in range(2))
    owner = (spot_x + ring) % 4 * 2 + (spot_low + pair) % 2
    strip = row // (local_columns * tile_rows) * tile_rows + row % tile_rows
    place = strip * columns + owner * local_columns + row // tile_rows % local_columns
    place = jnp.where(row < piece, place, -1).astype(jnp.int32)
    cell = lax.iota(jnp.int32, tokens)
    perm = (place[:, None] == cell[None, :]).astype(BF16)
    perm_back = (cell[:, None] == place[None, :]).astype(BF16)
    hot = (cell[:, None] % columns // TILE_W == lax.iota(jnp.int32, 128)[None, :]).astype(BF16)

    own_mask = lax.dynamic_slice_in_dim(block_mask, seq_place, 1, 1).reshape(-1, OFFSETS)
    bias = mask_bias(window, own_mask, seq_place, row_tiles)

    def whole(shape):
        return pl.BlockSpec(shape, lambda h: (0,) * len(shape))

    q_spec = pl.BlockSpec((tokens, HEAD_DIM), lambda h: (0, h))
    kv_spec = pl.BlockSpec((2, tokens, HEAD_DIM), lambda h: (0, 0, h))
    key_specs = [pl.BlockSpec((None, tokens, HEAD_DIM), lambda h: (0, 0, h)), q_spec, q_spec]
    value_specs = [pl.BlockSpec((None, tokens, HEAD_DIM), lambda h: (1, 0, h)), q_spec, q_spec]
    p_spec = pl.BlockSpec((1, 3, tokens, tokens), lambda h: (h, 0, 0, 0))
    weights = ((2, 1), (2, 0), (1, 0), (3, 1), (1, 1), (3, 0), (0, 1), (0, 0))
    ring, pair = (np.array([w[i] for w in weights], np.int32) for i in range(2))
    chips = (spot_z + ring) % 4 * 2 + (spot_y + pair) % 2
    order = jnp.concatenate([chips, core]).astype(jnp.int32)

    pairs = heads * tokens * 3 * tokens
    (probs,) = kernel(
        scores_kernel,
        [((heads, 3, tokens, tokens), BF16)],
        [flat_q, *halos[0], bias, hot],
        [
            q_spec,
            *key_specs,
            pl.BlockSpec((1, 3, columns, 128), lambda h: (h, 0, 0, 0)),
            whole((tokens, 128)),
        ],
        [p_spec],
        grid=(heads,),
        after=[perm, perm_back, order],
        flops=pairs * 1000,
        moved=6 << 20,
    )
    (attended,) = kernel(
        attend_kernel,
        [((slots, channels), BF16)],
        [probs, *halos[1], perm],
        [p_spec, *value_specs, whole((slots, tokens))],
        [pl.BlockSpec((slots, HEAD_DIM), lambda h: (0, h))],
        grid=(heads,),
        after=last_hops,
        flops=pairs * 500,
        moved=6 << 20,
    )
    far_grad = seq_shift(all_grad, 0, 0, 1)
    far_attended = seq_shift(attended, 0, 0, 1)

    broad = model_width // 4
    mixed = kernel(
        project_kernel,
        [((room, model_width), BF16)] * 8,
        [attended, out_weight],
        [whole((slots, channels)), pl.BlockSpec((channels, broad), lambda i: (0, i))],
        [pl.BlockSpec((room, broad), lambda i: (0, i))] * 8,
        grid=(4,),
        flops=slots * model_width * channels * 3,
        moved=12 << 20,
    )
    mixed = dict(zip(BLOCKS, mixed))
    mixed_far = hop(tensor_shift, (mixed[2, 1], mixed[2, 0]))
    mixed_near = hop(tensor_shift, (mixed[1, 0], mixed[3, 1]))

    narrow = model_width // row_tiles
    weight = kernel(
        weight_kernel,
        [((narrow, channels), BF16)] * 8,
        [order, all_grad, far_grad, attended, far_attended],
        [SCALAR] + [VECTOR] * 4,
        after=[mixed[0, 0]],
        flops=slots * model_width * channels * 2,
        moved=6 << 20,
    )
    weight = dict(zip(weights, weight))
    weight_far = hop(seq_shift, (weight[2, 1], weight[2, 0]))
    weight_near = hop(seq_shift, (weight[1, 0], weight[3, 1]))

    (grad_attn,) = kernel(
        attn_grad_kernel,
        [((slots, channels), BF16)],
        [out_weight, all_grad],
        [
            pl.BlockSpec((channels, broad), lambda i: (0, i)),
            pl.BlockSpec((slots, broad), lambda i: (0, i)),
        ],
        [whole((slots, channels))],
        grid=(4,),
        after=[weight[0, 0]],
        flops=slots * model_width * channels * 3,
        moved=12 << 20,
        scratch=[pltpu.VMEM((slots, channels), F32)],
    )

    def differentiate(first, count, after):
        def spec(shape, at):
            def index(h):
                return tuple(h + first if i == at else 0 for i in range(len(shape)))

            return pl.BlockSpec(shape, index)

        def own(which):
            return pl.BlockSpec((None, tokens, HEAD_DIM), lambda h: (which, 0, h + first))

        width = count * HEAD_DIM
        one = spec((tokens, HEAD_DIM), 1)
        halo = ((2, tokens, width), BF16)
        return kernel(
            backward_kernel,
            [((tokens, width), BF16), (halo[0], F32), halo, halo],
            [flat_q, *halos[0], *halos[1], probs, grad_attn, perm_back],
            [
                one,
                own(0),
                one,
                one,
                own(1),
                one,
                one,
                spec((1, 3, tokens, tokens), 0),
                spec((slots, HEAD_DIM), 1),
                whole((tokens, slots)),
            ],
            [q_spec, kv_spec, kv_spec, kv_spec],
            grid=(count,),
            after=after,
            flops=pairs * 2000 * count // heads,
            moved=2 * count << 20,
        )

    def send_halo(grad_up, grad_down):
        from_below = lax.ppermute(grad_up, "seq", back)
        from_above = lax.ppermute(grad_down, "seq", onward)
        return from_below, from_above

    split = (heads + 1) // 2
    gq_a, own_a, *ends_a = differentiate(0, split, [])
    halo_a = send_halo(*ends_a)
    gq_b, own_b, *ends_b = differentiate(split, heads - split, ends_a[:1])
    halo_b = send_halo(*ends_b)

    def relayed(kept, came, shift):
        sums = [added(k, c).astype(BF16) for k, c in zip(kept, came)]
        return hop(shift, sums)

    def side(shift, *terms):
        total = added(*terms).astype(BF16)
        return shift(total, 0, 1)

    mixed_sums = relayed((mixed[1, 1], mixed[3, 0]), mixed_far, tensor_shift)
    weight_sums = relayed((weight[1, 1], weight[3, 0]), weight_far, seq_shift)
    mixed_side = side(tensor_shift, mixed[0, 1], mixed_near[1], mixed_sums[0])
    weight_side = side(seq_shift, weight[0, 1], weight_near[1], weight_sums[0])
    (layer_out,) = kernel(
        mixed_kernel,
        [((frames, local_columns, tile_rows, model_width), BF16)],
        [mixed[0, 0], mixed_near[0], mixed_sums[1], mixed_side],
        moved=3 << 20,
    )
    grad_weight = added(weight[0, 0], weight_near[0], weight_sums[1], weight_side).astype(BF16)
    (grad_kv,) = kernel(
        total_kernel,
        [((2, tokens, channels), BF16)],
        [own_a, *halo_a, own_b, *halo_b],
        after=[layer_out],
        moved=5 << 20,
    )
    grad_q = jnp.concatenate([gq_a, gq_b], axis=1)
    return (
        layer_out.transpose(0, 2, 1, 3),
        grad_q.reshape(queries.shape),
        grad_kv.reshape(keys_values.shape),
        grad_weight.T,
    )


def solution(mesh):
    return jax.shard_map(
        layer,
        mesh=mesh,
        in_specs=(
            P(None, "seq", None, "tensor"),
            P(None, None, "seq", None, "tensor"),
            P("tensor", None),
            P(None, "seq", "tensor", None),
            P("tensor", None),
            P(),
        ),
        out_specs=(
            P(None, "seq", "tensor", None),
            P(None, "seq", None, "tensor"),
            P(None, None, "seq", None, "tensor"),
            P("tensor", "seq"),
        ),
        check_vma=False,
    )
```

```python
import jax
import jax.numpy as jnp
import numpy as np
from jax import lax
from jax.experimental import pallas as pl
from jax.experimental.pallas import tpu as pltpu
from jax.sharding import PartitionSpec as P

HEAD_DIM = 128
TILE_W = 8
REACH_W = 3
OFFSETS = 63
SCALE = HEAD_DIM ** (-0.5)
OUTSIDE = -1e30
F32 = jnp.float32
BF16 = jnp.bfloat16


def dot(a, b, dims):
    return lax.dot_general(a, b, (dims, ((), ())), preferred_element_type=F32)


def tensor_shift(value, dx, dy):
    pairs = [
        (x * 2 + y, (x + dx) % 4 * 2 + (y + dy) % 2) for x in range(4) for y in range(2)
    ]
    return lax.ppermute(value, "tensor", pairs)


def seq_shift(value, dz, dy, core=0):
    pairs = [
        ((z * 2 + y) * 2 + c, ((z + dz) % 4 * 2 + (y + dy) % 2) * 2 + (c + core) % 2)
        for z in range(4)
        for y in range(2)
        for c in range(2)
    ]
    return lax.ppermute(value, "seq", pairs)


def added(*terms):
    total = terms[0].astype(F32)
    for term in terms[1:]:
        total = total + term.astype(F32)
    return total


BLOCKS = ((0, 0), (1, 0), (3, 0), (0, 1), (3, 1), (1, 1), (2, 0), (2, 1))


def gathered(own, shift):
    c01 = shift(own, 0, 1)
    c10 = shift(own, -1, 0)
    c30 = shift(own, 1, 0)
    c20 = shift(c10, -1, 0)
    c11 = shift(c01, -1, 0)
    c31 = shift(c01, 1, 0)
    c21 = shift(c31, 1, 0)
    return jnp.concatenate([own, c10, c30, c01, c31, c11, c20, c21], axis=0), [c10, c31]


ROOM = 24 << 20
ANYWHERE = pl.BlockSpec(memory_space=pl.ANY)


def kernel(body, outs, args, specs=None, out_specs=None, grid=(), after=(), flops=0, moved=0, scratch=()):
    count = len(args)

    def run(*refs):
        return body(*refs[:count], *refs[count + len(after) :])

    vector = pl.BlockSpec(memory_space=pltpu.VMEM)
    specs = [vector] * count if specs is None else specs
    out_specs = [vector] * len(outs) if out_specs is None else out_specs
    return pl.pallas_call(
        run,
        grid=grid,
        in_specs=[*specs, *[ANYWHERE] * len(after)],
        out_specs=out_specs,
        out_shape=[jax.ShapeDtypeStruct(shape, kind) for shape, kind in outs],
        scratch_shapes=scratch,
        compiler_params=pltpu.CompilerParams(vmem_limit_bytes=ROOM),
        cost_estimate=pl.CostEstimate(flops=flops, transcendentals=0, bytes_accessed=moved),
    )(*args, *after)


def mixed_kernel(*refs):
    out_ref = refs[-1]
    total = added(*[r[...] for r in refs[:-1]])
    frames, columns, rows, _ = out_ref.shape
    for f in range(frames):
        for c in range(columns):
            start = (f * columns + c) * rows
            out_ref[f, c] = total[start : start + rows].astype(BF16)


SCALAR = pl.BlockSpec(memory_space=pltpu.SMEM)
VECTOR = pl.BlockSpec(memory_space=pltpu.VMEM)


def hop(shift, arrays):
    return [shift(arrays[i], 1 - 2 * i, 0) for i in range(2)]


def scores_kernel(q_ref, own_ref, up_ref, down_ref, bias_ref, hot_ref, p_ref):
    qa = jnp.concatenate([q_ref[...], hot_ref[...]], axis=1)
    scores = []
    for b, ref in enumerate((up_ref, own_ref, down_ref)):
        bias = jnp.concatenate([bias_ref[0, b]] * 9, axis=0).astype(BF16)
        ka = jnp.concatenate([ref[...], bias], axis=1)
        scores.append(dot(ka, qa, ((1,), (1,))))
    top = jnp.max(scores[0], axis=0, keepdims=True)
    for s in scores[1:]:
        top = jnp.maximum(top, jnp.max(s, axis=0, keepdims=True))
    weights = [jnp.exp((s - top) * SCALE) for s in scores]
    total = jnp.sum(weights[0], axis=0, keepdims=True)
    for w in weights[1:]:
        total = total + jnp.sum(w, axis=0, keepdims=True)
    inverse = 1.0 / total
    for b in range(3):
        p_ref[0, b] = (weights[b] * inverse).astype(BF16)


def attend_kernel(p_ref, own_ref, up_ref, down_ref, perm_ref, att_ref):
    attended = None
    for b, ref in enumerate((up_ref, own_ref, down_ref)):
        part = dot(ref[...], p_ref[0, b], ((0,), (0,)))
        attended = part if attended is None else attended + part
    att_ref[...] = dot(perm_ref[...], attended.astype(BF16), ((1,), (1,))).astype(BF16)


def backward_kernel(q_ref, *refs):
    keys, values = (refs[1], refs[0], refs[2]), (refs[4], refs[3], refs[5])
    p_ref, ga_ref, perm_ref, gq_ref, gown_ref, gup_ref, gdown_ref = refs[6:]
    q = q_ref[...]
    g = dot(perm_ref[...], ga_ref[...], ((1,), (0,))).astype(BF16)
    outs = (gup_ref, gown_ref, gdown_ref)
    grads = []
    delta = None
    for b in range(3):
        gp = dot(values[b][...], g, ((1,), (1,)))
        part = jnp.sum(p_ref[0, b].astype(F32) * gp, axis=0, keepdims=True)
        delta = part if delta is None else delta + part
        grads.append(gp)
    gq = None
    for b in range(3):
        probs = p_ref[0, b]
        ds = (probs.astype(F32) * (grads[b] - delta) * SCALE).astype(BF16)
        outs[b][0] = dot(ds, q, ((1,), (0,))).astype(outs[b].dtype)
        outs[b][1] = dot(probs, g, ((1,), (0,))).astype(outs[b].dtype)
        part = dot(keys[b][...], ds, ((0,), (0,)))
        gq = part if gq is None else gq + part
    gq_ref[...] = gq.T.astype(BF16)


def total_kernel(*refs):
    out_ref = refs[-1]
    start = 0
    for i in range(0, len(refs) - 1, 3):
        part = added(refs[i][...], refs[i + 1][...], refs[i + 2][...]).astype(BF16)
        out_ref[:, :, start : start + part.shape[2]] = part
        start += part.shape[2]


def weight_kernel(order_ref, g_ref, far_g_ref, att_ref, far_att_ref, *outs):
    attended = jnp.concatenate([att_ref[...], far_att_ref[...]], axis=0)
    core = order_ref[len(outs)]
    rows = outs[0].shape[0]
    lanes = 128
    wide = -(-rows // lanes) * lanes
    for i, out_ref in enumerate(outs):
        start = order_ref[i] * (2 * rows) + core * (2 * rows - wide)
        columns = pl.ds(pl.multiple_of(start, lanes), wide)
        turned = jnp.concatenate([g_ref[:, columns].T, far_g_ref[:, columns].T], axis=1)
        turned = jnp.where(core == 0, turned[:rows], turned[wide - rows :])
        out_ref[...] = dot(turned, attended, ((1,), (0,))).astype(BF16)


STEPS = 4


def project_kernel(att_ref, w_ref, *outs):
    room = outs[0].shape[0]
    width = w_ref.shape[1] // STEPS
    for i in range(STEPS):
        columns = slice(i * width, (i + 1) * width)
        mixed = dot(att_ref[...], w_ref[:, columns], ((1,), (0,)))
        for k, out_ref in enumerate(outs):
            out_ref[:, columns] = mixed[k * room : (k + 1) * room].astype(BF16)


def attn_grad_kernel(w_ref, g_ref, ga_ref):
    width = w_ref.shape[1] // STEPS
    total = None
    for i in range(STEPS):
        columns = slice(i * width, (i + 1) * width)
        part = dot(g_ref[:, columns], w_ref[:, columns], ((1,), (1,)))
        total = part if total is None else total + part
    ga_ref[...] = total.astype(BF16)


def mask_bias(window, own_mask, seq_place, row_tiles):
    heads = window.shape[0]
    columns = own_mask.shape[0]
    rows = own_mask.reshape(columns, 3, 3, 7)[:, 1]
    query = np.arange(columns)
    delta = query[:, None] - query[None, :]
    pick = (delta[:, :, None] + REACH_W == np.arange(7)).astype(np.int32)
    bits = jnp.sum(rows.transpose(1, 0, 2)[:, None] * pick[None], axis=-1)
    dh = jnp.arange(3, dtype=jnp.int32) - 1
    tile_row = dh + seq_place
    row_ok = (tile_row >= 0) & (tile_row < row_tiles)
    inside = (jnp.abs(dh)[None, :] <= window[:, 1:2]) & row_ok[None, :] & (window[:, :1] >= 0)
    near = np.abs(delta)[None] <= window[:, 2][:, None, None]
    ok = inside[:, :, None, None] & near[:, None] & (bits > 0)[None]
    bias = jnp.where(ok, 0.0, OUTSIDE).astype(F32)
    bias = jnp.pad(bias, ((0, 0), (0, 0), (0, 0), (0, 128 - columns)))
    wide = jnp.broadcast_to(bias[:, :, :, None], (heads, 3, columns, TILE_W, 128))
    return wide.reshape(heads, 3, columns * TILE_W, 128)


def layer(queries, keys_values, out_weight, grad_out, window, block_mask):
    frames, tile_rows, columns, channels = queries.shape
    model_width = grad_out.shape[3]
    local_columns = grad_out.shape[2]
    tokens = frames * tile_rows * columns
    heads = channels // HEAD_DIM
    strips = frames * tile_rows
    row_tiles = lax.axis_size("seq")
    seq_place = lax.axis_index("seq")
    tensor_place = lax.axis_index("tensor")
    spot_z, spot_y, core = seq_place // 4, seq_place // 2 % 2, seq_place % 2
    spot_x, spot_low = tensor_place // 2, tensor_place % 2
    core = core[None].astype(jnp.int32)

    onward = [(i, i + 1) for i in range(row_tiles - 1)]
    back = [(i + 1, i) for i in range(row_tiles - 1)]
    flat_q = queries.reshape(tokens, channels)
    flat_kv = keys_values.reshape(2, tokens, channels)
    halos = []
    for i in range(2):
        up = lax.ppermute(flat_kv[i], "seq", onward)
        down = lax.ppermute(flat_kv[i], "seq", back)
        halos.append([flat_kv, up, down])

    piece = strips * local_columns
    room = -(-piece // 16) * 16
    own_grad = grad_out.transpose(0, 2, 1, 3).reshape(piece, model_width)
    own_grad = jnp.pad(own_grad, ((0, room - piece), (0, 0)))
    all_grad, last_hops = gathered(own_grad, tensor_shift)
    slots = 8 * room

    row = np.arange(slots) % room
    ring, pair = (np.repeat([b[i] for b in BLOCKS], room).astype(np.int32) for i in range(2))
    owner = (spot_x + ring) % 4 * 2 + (spot_low + pair) % 2
    strip = row // (local_columns * tile_rows) * tile_rows + row % tile_rows
    place = strip * columns + owner * local_columns + row // tile_rows % local_columns
    place = jnp.where(row < piece, place, -1).astype(jnp.int32)
    cell = lax.iota(jnp.int32, tokens)
    perm = (place[:, None] == cell[None, :]).astype(BF16)
    perm_back = (cell[:, None] == place[None, :]).astype(BF16)
    hot = (cell[:, None] % columns // TILE_W == lax.iota(jnp.int32, 128)[None, :]).astype(BF16)

    own_mask = lax.dynamic_slice_in_dim(block_mask, seq_place, 1, 1).reshape(-1, OFFSETS)
    bias = mask_bias(window, own_mask, seq_place, row_tiles)

    def whole(shape):
        return pl.BlockSpec(shape, lambda h: (0,) * len(shape))

    q_spec = pl.BlockSpec((tokens, HEAD_DIM), lambda h: (0, h))
    kv_spec = pl.BlockSpec((2, tokens, HEAD_DIM), lambda h: (0, 0, h))
    key_specs = [pl.BlockSpec((None, tokens, HEAD_DIM), lambda h: (0, 0, h)), q_spec, q_spec]
    value_specs = [pl.BlockSpec((None, tokens, HEAD_DIM), lambda h: (1, 0, h)), q_spec, q_spec]
    p_spec = pl.BlockSpec((1, 3, tokens, tokens), lambda h: (h, 0, 0, 0))
    weights = ((2, 1), (2, 0), (1, 0), (3, 1), (1, 1), (3, 0), (0, 1), (0, 0))
    ring, pair = (np.array([w[i] for w in weights], np.int32) for i in range(2))
    chips = (spot_z + ring) % 4 * 2 + (spot_y + pair) % 2
    order = jnp.concatenate([chips, core]).astype(jnp.int32)

    pairs = heads * tokens * 3 * tokens
    (probs,) = kernel(
        scores_kernel,
        [((heads, 3, tokens, tokens), BF16)],
        [flat_q, *halos[0], bias, hot],
        [
            q_spec,
            *key_specs,
            pl.BlockSpec((1, 3, columns, 128), lambda h: (h, 0, 0, 0)),
            whole((tokens, 128)),
        ],
        [p_spec],
        grid=(heads,),
        after=[perm, perm_back, order],
        flops=pairs * 1000,
        moved=6 << 20,
    )
    (attended,) = kernel(
        attend_kernel,
        [((slots, channels), BF16)],
        [probs, *halos[1], perm],
        [p_spec, *value_specs, whole((slots, tokens))],
        [pl.BlockSpec((slots, HEAD_DIM), lambda h: (0, h))],
        grid=(heads,),
        after=last_hops,
        flops=pairs * 500,
        moved=6 << 20,
    )
    far_grad = seq_shift(all_grad, 0, 0, 1)
    far_attended = seq_shift(attended, 0, 0, 1)

    mixed = kernel(
        project_kernel,
        [((room, model_width), BF16)] * 8,
        [attended, out_weight],
        flops=slots * model_width * channels * 3,
        moved=12 << 20,
    )
    mixed = dict(zip(BLOCKS, mixed))
    mixed_far = hop(tensor_shift, (mixed[2, 1], mixed[2, 0]))
    mixed_near = hop(tensor_shift, (mixed[1, 0], mixed[3, 1]))

    (grad_attn,) = kernel(
        attn_grad_kernel,
        [((slots, channels), BF16)],
        [out_weight, all_grad],
        after=[mixed[0, 0]],
        flops=slots * model_width * channels * 3,
        moved=12 << 20,
    )

    narrow = model_width // row_tiles
    weight = kernel(
        weight_kernel,
        [((narrow, channels), BF16)] * 8,
        [order, all_grad, far_grad, attended, far_attended],
        [SCALAR] + [VECTOR] * 4,
        after=[grad_attn],
        flops=slots * model_width * channels * 2,
        moved=6 << 20,
    )
    weight = dict(zip(weights, weight))
    weight_far = hop(seq_shift, (weight[2, 1], weight[2, 0]))
    weight_near = hop(seq_shift, (weight[1, 0], weight[3, 1]))

    def differentiate(first, count, after):
        def spec(shape, at):
            def index(h):
                return tuple(h + first if i == at else 0 for i in range(len(shape)))

            return pl.BlockSpec(shape, index)

        def own(which):
            return pl.BlockSpec((None, tokens, HEAD_DIM), lambda h: (which, 0, h + first))

        width = count * HEAD_DIM
        one = spec((tokens, HEAD_DIM), 1)
        halo = ((2, tokens, width), BF16)
        return kernel(
            backward_kernel,
            [((tokens, width), BF16), (halo[0], F32), halo, halo],
            [flat_q, *halos[0], *halos[1], probs, grad_attn, perm_back],
            [
                one,
                own(0),
                one,
                one,
                own(1),
                one,
                one,
                spec((1, 3, tokens, tokens), 0),
                spec((slots, HEAD_DIM), 1),
                whole((tokens, slots)),
            ],
            [q_spec, kv_spec, kv_spec, kv_spec],
            grid=(count,),
            after=after,
            flops=pairs * 2000 * count // heads,
            moved=2 * count << 20,
        )

    def send_halo(grad_up, grad_down):
        from_below = lax.ppermute(grad_up, "seq", back)
        from_above = lax.ppermute(grad_down, "seq", onward)
        return from_below, from_above

    split = (heads + 1) // 2
    gq_a, own_a, *ends_a = differentiate(0, split, [weight[0, 0]])
    halo_a = send_halo(*ends_a)
    gq_b, own_b, *ends_b = differentiate(split, heads - split, ends_a[:1])
    halo_b = send_halo(*ends_b)

    def relayed(kept, came, shift):
        sums = [added(k, c).astype(BF16) for k, c in zip(kept, came)]
        return hop(shift, sums)

    def side(shift, *terms):
        total = added(*terms).astype(BF16)
        return shift(total, 0, 1)

    mixed_sums = relayed((mixed[1, 1], mixed[3, 0]), mixed_far, tensor_shift)
    weight_sums = relayed((weight[1, 1], weight[3, 0]), weight_far, seq_shift)
    mixed_side = side(tensor_shift, mixed[0, 1], mixed_near[1], mixed_sums[0])
    weight_side = side(seq_shift, weight[0, 1], weight_near[1], weight_sums[0])
    (layer_out,) = kernel(
        mixed_kernel,
        [((frames, local_columns, tile_rows, model_width), BF16)],
        [mixed[0, 0], mixed_near[0], mixed_sums[1], mixed_side],
        moved=3 << 20,
    )
    grad_weight = added(weight[0, 0], weight_near[0], weight_sums[1], weight_side).astype(BF16)
    (grad_kv,) = kernel(
        total_kernel,
        [((2, tokens, channels), BF16)],
        [own_a, *halo_a, own_b, *halo_b],
        after=[layer_out],
        moved=5 << 20,
    )
    grad_q = jnp.concatenate([gq_a, gq_b], axis=1)
    return (
        layer_out.transpose(0, 2, 1, 3),
        grad_q.reshape(queries.shape),
        grad_kv.reshape(keys_values.shape),
        grad_weight.T,
    )


def solution(mesh):
    return jax.shard_map(
        layer,
        mesh=mesh,
        in_specs=(
            P(None, "seq", None, "tensor"),
            P(None, None, "seq", None, "tensor"),
            P("tensor", None),
            P(None, "seq", "tensor", None),
            P("tensor", None),
            P(),
        ),
        out_specs=(
            P(None, "seq", "tensor", None),
            P(None, "seq", None, "tensor"),
            P(None, None, "seq", None, "tensor"),
            P("tensor", "seq"),
        ),
        check_vma=False,
    )
```

```python
import jax
import jax.numpy as jnp
import numpy as np
from jax import lax
from jax.experimental import pallas as pl
from jax.experimental.pallas import tpu as pltpu
from jax.sharding import PartitionSpec as P

HEAD_DIM = 128
TILE_W = 8
REACH_W = 3
OFFSETS = 63
SCALE = HEAD_DIM ** (-0.5)
OUTSIDE = -1e30
F32 = jnp.float32
BF16 = jnp.bfloat16


def dot(a, b, dims):
    return lax.dot_general(a, b, (dims, ((), ())), preferred_element_type=F32)


def tensor_shift(value, dx, dy):
    pairs = [
        (x * 2 + y, (x + dx) % 4 * 2 + (y + dy) % 2) for x in range(4) for y in range(2)
    ]
    return lax.ppermute(value, "tensor", pairs)


def seq_shift(value, dz, dy, core=0):
    pairs = [
        ((z * 2 + y) * 2 + c, ((z + dz) % 4 * 2 + (y + dy) % 2) * 2 + (c + core) % 2)
        for z in range(4)
        for y in range(2)
        for c in range(2)
    ]
    return lax.ppermute(value, "seq", pairs)


def added(*terms):
    total = terms[0].astype(F32)
    for term in terms[1:]:
        total = total + term.astype(F32)
    return total


BLOCKS = ((0, 0), (1, 0), (3, 0), (0, 1), (3, 1), (1, 1), (2, 0), (2, 1))


def gathered(own, shift):
    c01 = shift(own, 0, 1)
    c10 = shift(own, -1, 0)
    c30 = shift(own, 1, 0)
    c20 = shift(c10, -1, 0)
    c11 = shift(c01, -1, 0)
    c31 = shift(c01, 1, 0)
    c21 = shift(c31, 1, 0)
    return jnp.concatenate([own, c10, c30, c01, c31, c11, c20, c21], axis=0), [c10, c31]


ROOM = 24 << 20
ANYWHERE = pl.BlockSpec(memory_space=pl.ANY)


def kernel(body, outs, args, specs=None, out_specs=None, grid=(), after=(), flops=0, moved=0, scratch=()):
    count = len(args)

    def run(*refs):
        return body(*refs[:count], *refs[count + len(after) :])

    vector = pl.BlockSpec(memory_space=pltpu.VMEM)
    specs = [vector] * count if specs is None else specs
    out_specs = [vector] * len(outs) if out_specs is None else out_specs
    return pl.pallas_call(
        run,
        grid=grid,
        in_specs=[*specs, *[ANYWHERE] * len(after)],
        out_specs=out_specs,
        out_shape=[jax.ShapeDtypeStruct(shape, kind) for shape, kind in outs],
        scratch_shapes=scratch,
        compiler_params=pltpu.CompilerParams(vmem_limit_bytes=ROOM),
        cost_estimate=pl.CostEstimate(flops=flops, transcendentals=0, bytes_accessed=moved),
    )(*args, *after)


def mixed_kernel(*refs):
    out_ref = refs[-1]
    total = added(*[r[...] for r in refs[:-1]])
    frames, columns, rows, _ = out_ref.shape
    for f in range(frames):
        for c in range(columns):
            start = (f * columns + c) * rows
            out_ref[f, c] = total[start : start + rows].astype(BF16)


SCALAR = pl.BlockSpec(memory_space=pltpu.SMEM)
VECTOR = pl.BlockSpec(memory_space=pltpu.VMEM)


def hop(shift, arrays):
    return [shift(arrays[i], 1 - 2 * i, 0) for i in range(2)]


def scores_kernel(q_ref, own_ref, up_ref, down_ref, bias_ref, hot_ref, p_ref):
    qa = jnp.concatenate([q_ref[...], hot_ref[...]], axis=1)
    scores = []
    for b, ref in enumerate((up_ref, own_ref, down_ref)):
        bias = jnp.concatenate([bias_ref[0, b]] * 9, axis=0).astype(BF16)
        ka = jnp.concatenate([ref[...], bias], axis=1)
        scores.append(dot(ka, qa, ((1,), (1,))))
    top = jnp.max(scores[0], axis=0, keepdims=True)
    for s in scores[1:]:
        top = jnp.maximum(top, jnp.max(s, axis=0, keepdims=True))
    weights = [jnp.exp((s - top) * SCALE) for s in scores]
    total = jnp.sum(weights[0], axis=0, keepdims=True)
    for w in weights[1:]:
        total = total + jnp.sum(w, axis=0, keepdims=True)
    inverse = 1.0 / total
    for b in range(3):
        p_ref[0, b] = (weights[b] * inverse).astype(BF16)


def attend_kernel(p_ref, own_ref, up_ref, down_ref, perm_ref, att_ref):
    attended = None
    for b, ref in enumerate((up_ref, own_ref, down_ref)):
        part = dot(ref[...], p_ref[0, b], ((0,), (0,)))
        attended = part if attended is None else attended + part
    att_ref[...] = dot(perm_ref[...], attended.astype(BF16), ((1,), (1,))).astype(BF16)


def backward_kernel(q_ref, *refs):
    keys, values = (refs[1], refs[0], refs[2]), (refs[4], refs[3], refs[5])
    p_ref, ga_ref, perm_ref, gq_ref, gown_ref, gup_ref, gdown_ref = refs[6:]
    q = q_ref[...]
    g = dot(perm_ref[...], ga_ref[...], ((1,), (0,))).astype(BF16)
    outs = (gup_ref, gown_ref, gdown_ref)
    grads = []
    delta = None
    for b in range(3):
        gp = dot(values[b][...], g, ((1,), (1,)))
        part = jnp.sum(p_ref[0, b].astype(F32) * gp, axis=0, keepdims=True)
        delta = part if delta is None else delta + part
        grads.append(gp)
    gq = None
    for b in range(3):
        probs = p_ref[0, b]
        ds = (probs.astype(F32) * (grads[b] - delta) * SCALE).astype(BF16)
        outs[b][0] = dot(ds, q, ((1,), (0,))).astype(outs[b].dtype)
        outs[b][1] = dot(probs, g, ((1,), (0,))).astype(outs[b].dtype)
        part = dot(keys[b][...], ds, ((0,), (0,)))
        gq = part if gq is None else gq + part
    gq_ref[...] = gq.T.astype(BF16)


def total_kernel(*refs):
    out_ref = refs[-1]
    start = 0
    for i in range(0, len(refs) - 1, 3):
        part = added(refs[i][...], refs[i + 1][...], refs[i + 2][...]).astype(BF16)
        out_ref[:, :, start : start + part.shape[2]] = part
        start += part.shape[2]


def weight_kernel(order_ref, g_ref, far_g_ref, att_ref, far_att_ref, *outs):
    attended = jnp.concatenate([att_ref[...], far_att_ref[...]], axis=0)
    core = order_ref[len(outs)]
    rows = outs[0].shape[0]
    lanes = 128
    wide = -(-rows // lanes) * lanes
    for i, out_ref in enumerate(outs):
        start = order_ref[i] * (2 * rows) + core * (2 * rows - wide)
        columns = pl.ds(pl.multiple_of(start, lanes), wide)
        turned = jnp.concatenate([g_ref[:, columns].T, far_g_ref[:, columns].T], axis=1)
        turned = jnp.where(core == 0, turned[:rows], turned[wide - rows :])
        out_ref[...] = dot(turned, attended, ((1,), (0,))).astype(BF16)


STEPS = 4


def project_kernel(att_ref, w_ref, *outs):
    room = outs[0].shape[0]
    width = w_ref.shape[1] // STEPS
    for i in range(STEPS):
        columns = slice(i * width, (i + 1) * width)
        mixed = dot(att_ref[...], w_ref[:, columns], ((1,), (0,)))
        for k, out_ref in enumerate(outs):
            out_ref[:, columns] = mixed[k * room : (k + 1) * room].astype(BF16)


def attn_grad_kernel(w_ref, g_ref, ga_ref):
    width = w_ref.shape[1] // STEPS
    total = None
    for i in range(STEPS):
        columns = slice(i * width, (i + 1) * width)
        part = dot(g_ref[:, columns], w_ref[:, columns], ((1,), (1,)))
        total = part if total is None else total + part
    ga_ref[...] = total.astype(BF16)


def mask_bias(window, own_mask, seq_place, row_tiles):
    heads = window.shape[0]
    columns = own_mask.shape[0]
    rows = own_mask.reshape(columns, 3, 3, 7)[:, 1]
    query = np.arange(columns)
    delta = query[:, None] - query[None, :]
    pick = (delta[:, :, None] + REACH_W == np.arange(7)).astype(np.int32)
    bits = jnp.sum(rows.transpose(1, 0, 2)[:, None] * pick[None], axis=-1)
    dh = jnp.arange(3, dtype=jnp.int32) - 1
    tile_row = dh + seq_place
    row_ok = (tile_row >= 0) & (tile_row < row_tiles)
    inside = (jnp.abs(dh)[None, :] <= window[:, 1:2]) & row_ok[None, :] & (window[:, :1] >= 0)
    near = np.abs(delta)[None] <= window[:, 2][:, None, None]
    ok = inside[:, :, None, None] & near[:, None] & (bits > 0)[None]
    bias = jnp.where(ok, 0.0, OUTSIDE).astype(F32)
    bias = jnp.pad(bias, ((0, 0), (0, 0), (0, 0), (0, 128 - columns)))
    wide = jnp.broadcast_to(bias[:, :, :, None], (heads, 3, columns, TILE_W, 128))
    return wide.reshape(heads, 3, columns * TILE_W, 128)


def layer(queries, keys_values, out_weight, grad_out, window, block_mask):
    frames, tile_rows, columns, channels = queries.shape
    model_width = grad_out.shape[3]
    local_columns = grad_out.shape[2]
    tokens = frames * tile_rows * columns
    heads = channels // HEAD_DIM
    strips = frames * tile_rows
    row_tiles = lax.axis_size("seq")
    seq_place = lax.axis_index("seq")
    tensor_place = lax.axis_index("tensor")
    spot_z, spot_y, core = seq_place // 4, seq_place // 2 % 2, seq_place % 2
    spot_x, spot_low = tensor_place // 2, tensor_place % 2
    core = core[None].astype(jnp.int32)

    onward = [(i, i + 1) for i in range(row_tiles - 1)]
    back = [(i + 1, i) for i in range(row_tiles - 1)]
    flat_q = queries.reshape(tokens, channels)
    flat_kv = keys_values.reshape(2, tokens, channels)
    halos = []
    for i in range(2):
        up = lax.ppermute(flat_kv[i], "seq", onward)
        down = lax.ppermute(flat_kv[i], "seq", back)
        halos.append([flat_kv, up, down])

    piece = strips * local_columns
    room = -(-piece // 16) * 16
    own_grad = grad_out.transpose(0, 2, 1, 3).reshape(piece, model_width)
    own_grad = jnp.pad(own_grad, ((0, room - piece), (0, 0)))
    all_grad, last_hops = gathered(own_grad, tensor_shift)
    slots = 8 * room

    row = np.arange(slots) % room
    ring, pair = (np.repeat([b[i] for b in BLOCKS], room).astype(np.int32) for i in range(2))
    owner = (spot_x + ring) % 4 * 2 + (spot_low + pair) % 2
    strip = row // (local_columns * tile_rows) * tile_rows + row % tile_rows
    place = strip * columns + owner * local_columns + row // tile_rows % local_columns
    place = jnp.where(row < piece, place, -1).astype(jnp.int32)
    cell = lax.iota(jnp.int32, tokens)
    perm = (place[:, None] == cell[None, :]).astype(BF16)
    perm_back = (cell[:, None] == place[None, :]).astype(BF16)
    hot = (cell[:, None] % columns // TILE_W == lax.iota(jnp.int32, 128)[None, :]).astype(BF16)

    own_mask = lax.dynamic_slice_in_dim(block_mask, seq_place, 1, 1).reshape(-1, OFFSETS)
    bias = mask_bias(window, own_mask, seq_place, row_tiles)

    def whole(shape):
        return pl.BlockSpec(shape, lambda h: (0,) * len(shape))

    q_spec = pl.BlockSpec((tokens, HEAD_DIM), lambda h: (0, h))
    kv_spec = pl.BlockSpec((2, tokens, HEAD_DIM), lambda h: (0, 0, h))
    key_specs = [pl.BlockSpec((None, tokens, HEAD_DIM), lambda h: (0, 0, h)), q_spec, q_spec]
    value_specs = [pl.BlockSpec((None, tokens, HEAD_DIM), lambda h: (1, 0, h)), q_spec, q_spec]
    p_spec = pl.BlockSpec((1, 3, tokens, tokens), lambda h: (h, 0, 0, 0))
    weights = ((2, 1), (2, 0), (1, 0), (3, 1), (1, 1), (3, 0), (0, 1), (0, 0))
    ring, pair = (np.array([w[i] for w in weights], np.int32) for i in range(2))
    chips = (spot_z + ring) % 4 * 2 + (spot_y + pair) % 2
    order = jnp.concatenate([chips, core]).astype(jnp.int32)

    pairs = heads * tokens * 3 * tokens
    (probs,) = kernel(
        scores_kernel,
        [((heads, 3, tokens, tokens), BF16)],
        [flat_q, *halos[0], bias, hot],
        [
            q_spec,
            *key_specs,
            pl.BlockSpec((1, 3, columns, 128), lambda h: (h, 0, 0, 0)),
            whole((tokens, 128)),
        ],
        [p_spec],
        grid=(heads,),
        after=[perm, perm_back, order],
        flops=pairs * 1000,
        moved=6 << 20,
    )
    (attended,) = kernel(
        attend_kernel,
        [((slots, channels), BF16)],
        [probs, *halos[1], perm],
        [p_spec, *value_specs, whole((slots, tokens))],
        [pl.BlockSpec((slots, HEAD_DIM), lambda h: (0, h))],
        grid=(heads,),
        after=last_hops,
        flops=pairs * 500,
        moved=6 << 20,
    )
    far_grad = seq_shift(all_grad, 0, 0, 1)
    far_attended = seq_shift(attended, 0, 0, 1)

    mixed = kernel(
        project_kernel,
        [((room, model_width), BF16)] * 8,
        [attended, out_weight],
        flops=slots * model_width * channels * 3,
        moved=12 << 20,
    )
    mixed = dict(zip(BLOCKS, mixed))
    mixed_far = hop(tensor_shift, (mixed[2, 1], mixed[2, 0]))
    mixed_near = hop(tensor_shift, (mixed[1, 0], mixed[3, 1]))

    (grad_attn,) = kernel(
        attn_grad_kernel,
        [((slots, channels), BF16)],
        [out_weight, all_grad],
        after=[mixed[0, 0]],
        flops=slots * model_width * channels * 3,
        moved=12 << 20,
    )

    def differentiate(first, count, after):
        def spec(shape, at):
            def index(h):
                return tuple(h + first if i == at else 0 for i in range(len(shape)))

            return pl.BlockSpec(shape, index)

        def own(which):
            return pl.BlockSpec((None, tokens, HEAD_DIM), lambda h: (which, 0, h + first))

        width = count * HEAD_DIM
        one = spec((tokens, HEAD_DIM), 1)
        halo = ((2, tokens, width), BF16)
        return kernel(
            backward_kernel,
            [((tokens, width), BF16), (halo[0], F32), halo, halo],
            [flat_q, *halos[0], *halos[1], probs, grad_attn, perm_back],
            [
                one,
                own(0),
                one,
                one,
                own(1),
                one,
                one,
                spec((1, 3, tokens, tokens), 0),
                spec((slots, HEAD_DIM), 1),
                whole((tokens, slots)),
            ],
            [q_spec, kv_spec, kv_spec, kv_spec],
            grid=(count,),
            after=after,
            flops=pairs * 2000 * count // heads,
            moved=2 * count << 20,
        )

    def send_halo(grad_up, grad_down):
        from_below = lax.ppermute(grad_up, "seq", back)
        from_above = lax.ppermute(grad_down, "seq", onward)
        return from_below, from_above

    split = (heads + 1) // 2
    gq_a, own_a, *ends_a = differentiate(0, split, [])
    halo_a = send_halo(*ends_a)
    narrow = model_width // row_tiles
    weight = kernel(
        weight_kernel,
        [((narrow, channels), BF16)] * 8,
        [order, all_grad, far_grad, attended, far_attended],
        [SCALAR] + [VECTOR] * 4,
        after=ends_a[:1],
        flops=slots * model_width * channels * 2,
        moved=6 << 20,
    )
    weight = dict(zip(weights, weight))
    weight_far = hop(seq_shift, (weight[2, 1], weight[2, 0]))
    weight_near = hop(seq_shift, (weight[1, 0], weight[3, 1]))

    gq_b, own_b, *ends_b = differentiate(split, heads - split, [weight[0, 0]])
    halo_b = send_halo(*ends_b)

    def relayed(kept, came, shift):
        sums = [added(k, c).astype(BF16) for k, c in zip(kept, came)]
        return hop(shift, sums)

    def side(shift, *terms):
        total = added(*terms).astype(BF16)
        return shift(total, 0, 1)

    mixed_sums = relayed((mixed[1, 1], mixed[3, 0]), mixed_far, tensor_shift)
    weight_sums = relayed((weight[1, 1], weight[3, 0]), weight_far, seq_shift)
    mixed_side = side(tensor_shift, mixed[0, 1], mixed_near[1], mixed_sums[0])
    weight_side = side(seq_shift, weight[0, 1], weight_near[1], weight_sums[0])
    (layer_out,) = kernel(
        mixed_kernel,
        [((frames, local_columns, tile_rows, model_width), BF16)],
        [mixed[0, 0], mixed_near[0], mixed_sums[1], mixed_side],
        moved=3 << 20,
    )
    grad_weight = added(weight[0, 0], weight_near[0], weight_sums[1], weight_side).astype(BF16)
    (grad_kv,) = kernel(
        total_kernel,
        [((2, tokens, channels), BF16)],
        [own_a, *halo_a, own_b, *halo_b],
        after=[layer_out],
        moved=5 << 20,
    )
    grad_q = jnp.concatenate([gq_a, gq_b], axis=1)
    return (
        layer_out.transpose(0, 2, 1, 3),
        grad_q.reshape(queries.shape),
        grad_kv.reshape(keys_values.shape),
        grad_weight.T,
    )


def solution(mesh):
    return jax.shard_map(
        layer,
        mesh=mesh,
        in_specs=(
            P(None, "seq", None, "tensor"),
            P(None, None, "seq", None, "tensor"),
            P("tensor", None),
            P(None, "seq", "tensor", None),
            P("tensor", None),
            P(),
        ),
        out_specs=(
            P(None, "seq", "tensor", None),
            P(None, "seq", None, "tensor"),
            P(None, None, "seq", None, "tensor"),
            P("tensor", "seq"),
        ),
        check_vma=False,
    )
```

```python
import jax
import jax.numpy as jnp
import numpy as np
from jax import lax
from jax.experimental import pallas as pl
from jax.experimental.pallas import tpu as pltpu
from jax.sharding import PartitionSpec as P

HEAD_DIM = 128
TILE_W = 8
REACH_W = 3
OFFSETS = 63
SCALE = HEAD_DIM ** (-0.5)
OUTSIDE = -1e30
F32 = jnp.float32
BF16 = jnp.bfloat16


def dot(a, b, dims):
    return lax.dot_general(a, b, (dims, ((), ())), preferred_element_type=F32)


def tensor_shift(value, dx, dy):
    pairs = [
        (x * 2 + y, (x + dx) % 4 * 2 + (y + dy) % 2) for x in range(4) for y in range(2)
    ]
    return lax.ppermute(value, "tensor", pairs)


def seq_shift(value, dz, dy, core=0):
    pairs = [
        ((z * 2 + y) * 2 + c, ((z + dz) % 4 * 2 + (y + dy) % 2) * 2 + (c + core) % 2)
        for z in range(4)
        for y in range(2)
        for c in range(2)
    ]
    return lax.ppermute(value, "seq", pairs)


def added(*terms):
    total = terms[0].astype(F32)
    for term in terms[1:]:
        total = total + term.astype(F32)
    return total


BLOCKS = ((0, 0), (1, 0), (3, 0), (0, 1), (3, 1), (1, 1), (2, 0), (2, 1))


def gathered(own, shift):
    c01 = shift(own, 0, 1)
    c10 = shift(own, -1, 0)
    c30 = shift(own, 1, 0)
    c20 = shift(c10, -1, 0)
    c11 = shift(c01, -1, 0)
    c31 = shift(c01, 1, 0)
    c21 = shift(c31, 1, 0)
    return jnp.concatenate([own, c10, c30, c01, c31, c11, c20, c21], axis=0), [c10, c31]


ROOM = 24 << 20
ANYWHERE = pl.BlockSpec(memory_space=pl.ANY)


def kernel(body, outs, args, specs=None, out_specs=None, grid=(), after=(), flops=0, moved=0, scratch=()):
    count = len(args)

    def run(*refs):
        return body(*refs[:count], *refs[count + len(after) :])

    vector = pl.BlockSpec(memory_space=pltpu.VMEM)
    specs = [vector] * count if specs is None else specs
    out_specs = [vector] * len(outs) if out_specs is None else out_specs
    return pl.pallas_call(
        run,
        grid=grid,
        in_specs=[*specs, *[ANYWHERE] * len(after)],
        out_specs=out_specs,
        out_shape=[jax.ShapeDtypeStruct(shape, kind) for shape, kind in outs],
        scratch_shapes=scratch,
        compiler_params=pltpu.CompilerParams(vmem_limit_bytes=ROOM),
        cost_estimate=pl.CostEstimate(flops=flops, transcendentals=0, bytes_accessed=moved),
    )(*args, *after)


def mixed_kernel(*refs):
    out_ref = refs[-1]
    total = added(*[r[...] for r in refs[:-1]])
    frames, columns, rows, _ = out_ref.shape
    for f in range(frames):
        for c in range(columns):
            start = (f * columns + c) * rows
            out_ref[f, c] = total[start : start + rows].astype(BF16)


SCALAR = pl.BlockSpec(memory_space=pltpu.SMEM)
VECTOR = pl.BlockSpec(memory_space=pltpu.VMEM)


def hop(shift, arrays):
    return [shift(arrays[i], 1 - 2 * i, 0) for i in range(2)]


def scores_kernel(q_ref, own_ref, up_ref, down_ref, bias_ref, hot_ref, p_ref):
    qa = jnp.concatenate([q_ref[...], hot_ref[...]], axis=1)
    scores = []
    for b, ref in enumerate((up_ref, own_ref, down_ref)):
        bias = jnp.concatenate([bias_ref[0, b]] * 9, axis=0).astype(BF16)
        ka = jnp.concatenate([ref[...], bias], axis=1)
        scores.append(dot(ka, qa, ((1,), (1,))))
    top = jnp.max(scores[0], axis=0, keepdims=True)
    for s in scores[1:]:
        top = jnp.maximum(top, jnp.max(s, axis=0, keepdims=True))
    weights = [jnp.exp((s - top) * SCALE) for s in scores]
    total = jnp.sum(weights[0], axis=0, keepdims=True)
    for w in weights[1:]:
        total = total + jnp.sum(w, axis=0, keepdims=True)
    inverse = 1.0 / total
    for b in range(3):
        p_ref[0, b] = (weights[b] * inverse).astype(BF16)


def attend_kernel(p_ref, own_ref, up_ref, down_ref, perm_ref, att_ref):
    attended = None
    for b, ref in enumerate((up_ref, own_ref, down_ref)):
        part = dot(ref[...], p_ref[0, b], ((0,), (0,)))
        attended = part if attended is None else attended + part
    att_ref[...] = dot(perm_ref[...], attended.astype(BF16), ((1,), (1,))).astype(BF16)


def backward_kernel(q_ref, *refs):
    keys, values = (refs[1], refs[0], refs[2]), (refs[4], refs[3], refs[5])
    p_ref, ga_ref, perm_ref, gq_ref, gown_ref, gup_ref, gdown_ref = refs[6:]
    q = q_ref[...]
    g = dot(perm_ref[...], ga_ref[...], ((1,), (0,))).astype(BF16)
    outs = (gup_ref, gown_ref, gdown_ref)
    grads = []
    delta = None
    for b in range(3):
        gp = dot(values[b][...], g, ((1,), (1,)))
        part = jnp.sum(p_ref[0, b].astype(F32) * gp, axis=0, keepdims=True)
        delta = part if delta is None else delta + part
        grads.append(gp)
    gq = None
    for b in range(3):
        probs = p_ref[0, b]
        ds = (probs.astype(F32) * (grads[b] - delta) * SCALE).astype(BF16)
        outs[b][0] = dot(ds, q, ((1,), (0,))).astype(outs[b].dtype)
        outs[b][1] = dot(probs, g, ((1,), (0,))).astype(outs[b].dtype)
        part = dot(keys[b][...], ds, ((0,), (0,)))
        gq = part if gq is None else gq + part
    gq_ref[...] = gq.T.astype(BF16)


def total_kernel(*refs):
    out_ref = refs[-1]
    start = 0
    for i in range(0, len(refs) - 1, 3):
        part = added(refs[i][...], refs[i + 1][...], refs[i + 2][...]).astype(BF16)
        out_ref[:, :, start : start + part.shape[2]] = part
        start += part.shape[2]


def weight_kernel(order_ref, g_ref, far_g_ref, att_ref, far_att_ref, *outs):
    attended = jnp.concatenate([att_ref[...], far_att_ref[...]], axis=0)
    core = order_ref[len(outs)]
    rows = outs[0].shape[0]
    lanes = 128
    wide = -(-rows // lanes) * lanes
    for i, out_ref in enumerate(outs):
        start = order_ref[i] * (2 * rows) + core * (2 * rows - wide)
        columns = pl.ds(pl.multiple_of(start, lanes), wide)
        turned = jnp.concatenate([g_ref[:, columns].T, far_g_ref[:, columns].T], axis=1)
        turned = jnp.where(core == 0, turned[:rows], turned[wide - rows :])
        out_ref[...] = dot(turned, attended, ((1,), (0,))).astype(BF16)


STEPS = 4


def project_kernel(att_ref, w_ref, *outs):
    room = outs[0].shape[0]
    width = w_ref.shape[1] // STEPS
    for i in range(STEPS):
        columns = slice(i * width, (i + 1) * width)
        mixed = dot(att_ref[...], w_ref[:, columns], ((1,), (0,)))
        for k, out_ref in enumerate(outs):
            out_ref[:, columns] = mixed[k * room : (k + 1) * room].astype(BF16)


def attn_grad_kernel(w_ref, g_ref, ga_ref):
    width = w_ref.shape[1] // STEPS
    total = None
    for i in range(STEPS):
        columns = slice(i * width, (i + 1) * width)
        part = dot(g_ref[:, columns], w_ref[:, columns], ((1,), (1,)))
        total = part if total is None else total + part
    ga_ref[...] = total.astype(BF16)


def mask_bias(window, own_mask, seq_place, row_tiles):
    heads = window.shape[0]
    columns = own_mask.shape[0]
    rows = own_mask.reshape(columns, 3, 3, 7)[:, 1]
    query = np.arange(columns)
    delta = query[:, None] - query[None, :]
    pick = (delta[:, :, None] + REACH_W == np.arange(7)).astype(np.int32)
    bits = jnp.sum(rows.transpose(1, 0, 2)[:, None] * pick[None], axis=-1)
    dh = jnp.arange(3, dtype=jnp.int32) - 1
    tile_row = dh + seq_place
    row_ok = (tile_row >= 0) & (tile_row < row_tiles)
    inside = (jnp.abs(dh)[None, :] <= window[:, 1:2]) & row_ok[None, :] & (window[:, :1] >= 0)
    near = np.abs(delta)[None] <= window[:, 2][:, None, None]
    ok = inside[:, :, None, None] & near[:, None] & (bits > 0)[None]
    bias = jnp.where(ok, 0.0, OUTSIDE).astype(F32)
    bias = jnp.pad(bias, ((0, 0), (0, 0), (0, 0), (0, 128 - columns)))
    wide = jnp.broadcast_to(bias[:, :, :, None], (heads, 3, columns, TILE_W, 128))
    return wide.reshape(heads, 3, columns * TILE_W, 128)


def layer(queries, keys_values, out_weight, grad_out, window, block_mask):
    frames, tile_rows, columns, channels = queries.shape
    model_width = grad_out.shape[3]
    local_columns = grad_out.shape[2]
    tokens = frames * tile_rows * columns
    heads = channels // HEAD_DIM
    strips = frames * tile_rows
    row_tiles = lax.axis_size("seq")
    seq_place = lax.axis_index("seq")
    tensor_place = lax.axis_index("tensor")
    spot_z, spot_y, core = seq_place // 4, seq_place // 2 % 2, seq_place % 2
    spot_x, spot_low = tensor_place // 2, tensor_place % 2
    core = core[None].astype(jnp.int32)

    onward = [(i, i + 1) for i in range(row_tiles - 1)]
    back = [(i + 1, i) for i in range(row_tiles - 1)]
    flat_q = queries.reshape(tokens, channels)
    flat_kv = keys_values.reshape(2, tokens, channels)
    halos = []
    for i in range(2):
        up = lax.ppermute(flat_kv[i], "seq", onward)
        down = lax.ppermute(flat_kv[i], "seq", back)
        halos.append([flat_kv, up, down])

    piece = strips * local_columns
    room = -(-piece // 16) * 16
    own_grad = grad_out.transpose(0, 2, 1, 3).reshape(piece, model_width)
    own_grad = jnp.pad(own_grad, ((0, room - piece), (0, 0)))
    all_grad, last_hops = gathered(own_grad, tensor_shift)
    slots = 8 * room

    row = np.arange(slots) % room
    ring, pair = (np.repeat([b[i] for b in BLOCKS], room).astype(np.int32) for i in range(2))
    owner = (spot_x + ring) % 4 * 2 + (spot_low + pair) % 2
    strip = row // (local_columns * tile_rows) * tile_rows + row % tile_rows
    place = strip * columns + owner * local_columns + row // tile_rows % local_columns
    place = jnp.where(row < piece, place, -1).astype(jnp.int32)
    cell = lax.iota(jnp.int32, tokens)
    perm = (place[:, None] == cell[None, :]).astype(BF16)
    perm_back = (cell[:, None] == place[None, :]).astype(BF16)
    hot = (cell[:, None] % columns // TILE_W == lax.iota(jnp.int32, 128)[None, :]).astype(BF16)

    own_mask = lax.dynamic_slice_in_dim(block_mask, seq_place, 1, 1).reshape(-1, OFFSETS)
    bias = mask_bias(window, own_mask, seq_place, row_tiles)

    def whole(shape):
        return pl.BlockSpec(shape, lambda h: (0,) * len(shape))

    q_spec = pl.BlockSpec((tokens, HEAD_DIM), lambda h: (0, h))
    kv_spec = pl.BlockSpec((2, tokens, HEAD_DIM), lambda h: (0, 0, h))
    key_specs = [pl.BlockSpec((None, tokens, HEAD_DIM), lambda h: (0, 0, h)), q_spec, q_spec]
    value_specs = [pl.BlockSpec((None, tokens, HEAD_DIM), lambda h: (1, 0, h)), q_spec, q_spec]
    p_spec = pl.BlockSpec((1, 3, tokens, tokens), lambda h: (h, 0, 0, 0))
    firsts = ((2, 1), (2, 0))
    others = ((1, 1), (3, 0), (3, 1), (1, 0), (0, 1), (0, 0))

    def order_of(blocks):
        ring, pair = (np.array([w[i] for w in blocks], np.int32) for i in range(2))
        chips = (spot_z + ring) % 4 * 2 + (spot_y + pair) % 2
        return jnp.concatenate([chips, core]).astype(jnp.int32)

    orders = [order_of(firsts), order_of(others)]
    pairs = heads * tokens * 3 * tokens

    (probs,) = kernel(
        scores_kernel,
        [((heads, 3, tokens, tokens), BF16)],
        [flat_q, *halos[0], bias, hot],
        [
            q_spec,
            *key_specs,
            pl.BlockSpec((1, 3, columns, 128), lambda h: (h, 0, 0, 0)),
            whole((tokens, 128)),
        ],
        [p_spec],
        grid=(heads,),
        after=[perm, perm_back, *orders],
        flops=pairs * 1000,
        moved=6 << 20,
    )
    (attended,) = kernel(
        attend_kernel,
        [((slots, channels), BF16)],
        [probs, *halos[1], perm],
        [p_spec, *value_specs, whole((slots, tokens))],
        [pl.BlockSpec((slots, HEAD_DIM), lambda h: (0, h))],
        grid=(heads,),
        after=last_hops,
        flops=pairs * 500,
        moved=6 << 20,
    )
    far_grad = seq_shift(all_grad, 0, 0, 1)
    far_attended = seq_shift(attended, 0, 0, 1)

    mixed = kernel(
        project_kernel,
        [((room, model_width), BF16)] * 8,
        [attended, out_weight],
        flops=slots * model_width * channels * 3,
        moved=12 << 20,
    )
    mixed = dict(zip(BLOCKS, mixed))
    mixed_far = hop(tensor_shift, (mixed[2, 1], mixed[2, 0]))
    mixed_near = hop(tensor_shift, (mixed[1, 0], mixed[3, 1]))

    (grad_attn,) = kernel(
        attn_grad_kernel,
        [((slots, channels), BF16)],
        [out_weight, all_grad],
        after=[mixed[0, 0]],
        flops=slots * model_width * channels * 3,
        moved=12 << 20,
    )

    narrow = model_width // row_tiles

    def weight_blocks(blocks, order, after):
        return kernel(
            weight_kernel,
            [((narrow, channels), BF16)] * len(blocks),
            [order, all_grad, far_grad, attended, far_attended],
            [SCALAR] + [VECTOR] * 4,
            after=after,
            flops=slots * model_width * channels * 2 * len(blocks) // 8,
            moved=6 << 20,
        )

    weight = dict(zip(firsts, weight_blocks(firsts, orders[0], [grad_attn])))

    def differentiate(first, count, after):
        def spec(shape, at):
            def index(h):
                return tuple(h + first if i == at else 0 for i in range(len(shape)))

            return pl.BlockSpec(shape, index)

        def own(which):
            return pl.BlockSpec((None, tokens, HEAD_DIM), lambda h: (which, 0, h + first))

        width = count * HEAD_DIM
        one = spec((tokens, HEAD_DIM), 1)
        halo = ((2, tokens, width), BF16)
        return kernel(
            backward_kernel,
            [((tokens, width), BF16), (halo[0], F32), halo, halo],
            [flat_q, *halos[0], *halos[1], probs, grad_attn, perm_back],
            [
                one,
                own(0),
                one,
                one,
                own(1),
                one,
                one,
                spec((1, 3, tokens, tokens), 0),
                spec((slots, HEAD_DIM), 1),
                whole((tokens, slots)),
            ],
            [q_spec, kv_spec, kv_spec, kv_spec],
            grid=(count,),
            after=after,
            flops=pairs * 2000 * count // heads,
            moved=2 * count << 20,
        )

    def send_halo(grad_up, grad_down):
        from_below = lax.ppermute(grad_up, "seq", back)
        from_above = lax.ppermute(grad_down, "seq", onward)
        return from_below, from_above

    split = (heads + 1) // 2
    gq_a, own_a, *ends_a = differentiate(0, split, [weight[2, 1]])
    halo_a = send_halo(*ends_a)
    weight.update(zip(others, weight_blocks(others, orders[1], ends_a[:1])))
    weight_far = hop(seq_shift, (weight[2, 1], weight[2, 0]))
    weight_near = hop(seq_shift, (weight[1, 0], weight[3, 1]))

    gq_b, own_b, *ends_b = differentiate(split, heads - split, [weight[0, 0]])
    halo_b = send_halo(*ends_b)

    def relayed(kept, came, shift):
        sums = [added(k, c).astype(BF16) for k, c in zip(kept, came)]
        return hop(shift, sums)

    def side(shift, *terms):
        total = added(*terms).astype(BF16)
        return shift(total, 0, 1)

    mixed_sums = relayed((mixed[1, 1], mixed[3, 0]), mixed_far, tensor_shift)
    weight_sums = relayed((weight[1, 1], weight[3, 0]), weight_far, seq_shift)
    mixed_side = side(tensor_shift, mixed[0, 1], mixed_near[1], mixed_sums[0])
    weight_side = side(seq_shift, weight[0, 1], weight_near[1], weight_sums[0])
    (layer_out,) = kernel(
        mixed_kernel,
        [((frames, local_columns, tile_rows, model_width), BF16)],
        [mixed[0, 0], mixed_near[0], mixed_sums[1], mixed_side],
        moved=3 << 20,
    )
    grad_weight = added(weight[0, 0], weight_near[0], weight_sums[1], weight_side).astype(BF16)
    (grad_kv,) = kernel(
        total_kernel,
        [((2, tokens, channels), BF16)],
        [own_a, *halo_a, own_b, *halo_b],
        after=[layer_out],
        moved=5 << 20,
    )
    grad_q = jnp.concatenate([gq_a, gq_b], axis=1)
    return (
        layer_out.transpose(0, 2, 1, 3),
        grad_q.reshape(queries.shape),
        grad_kv.reshape(keys_values.shape),
        grad_weight.T,
    )


def solution(mesh):
    return jax.shard_map(
        layer,
        mesh=mesh,
        in_specs=(
            P(None, "seq", None, "tensor"),
            P(None, None, "seq", None, "tensor"),
            P("tensor", None),
            P(None, "seq", "tensor", None),
            P("tensor", None),
            P(),
        ),
        out_specs=(
            P(None, "seq", "tensor", None),
            P(None, "seq", None, "tensor"),
            P(None, None, "seq", None, "tensor"),
            P("tensor", "seq"),
        ),
        check_vma=False,
    )
```

```python
import jax
import jax.numpy as jnp
import numpy as np
from jax import lax
from jax.experimental import pallas as pl
from jax.experimental.pallas import tpu as pltpu
from jax.sharding import PartitionSpec as P

HEAD_DIM = 128
TILE_W = 8
REACH_W = 3
OFFSETS = 63
SCALE = HEAD_DIM ** (-0.5)
OUTSIDE = -1e30
F32 = jnp.float32
BF16 = jnp.bfloat16


def dot(a, b, dims):
    return lax.dot_general(a, b, (dims, ((), ())), preferred_element_type=F32)


def tensor_shift(value, dx, dy):
    pairs = [
        (x * 2 + y, (x + dx) % 4 * 2 + (y + dy) % 2) for x in range(4) for y in range(2)
    ]
    return lax.ppermute(value, "tensor", pairs)


def seq_shift(value, dz, dy, core=0):
    pairs = [
        ((z * 2 + y) * 2 + c, ((z + dz) % 4 * 2 + (y + dy) % 2) * 2 + (c + core) % 2)
        for z in range(4)
        for y in range(2)
        for c in range(2)
    ]
    return lax.ppermute(value, "seq", pairs)


def added(*terms):
    total = terms[0].astype(F32)
    for term in terms[1:]:
        total = total + term.astype(F32)
    return total


BLOCKS = ((0, 0), (1, 0), (3, 0), (0, 1), (3, 1), (1, 1), (2, 0), (2, 1))


def gathered(own, shift):
    c01 = shift(own, 0, 1)
    c10 = shift(own, -1, 0)
    c30 = shift(own, 1, 0)
    c20 = shift(c10, -1, 0)
    c11 = shift(c01, -1, 0)
    c31 = shift(c01, 1, 0)
    c21 = shift(c31, 1, 0)
    return [own, c10, c30, c01, c31, c11, c20, c21], [c10, c31]


ROOM = 24 << 20
ANYWHERE = pl.BlockSpec(memory_space=pl.ANY)


def kernel(body, outs, args, specs=None, out_specs=None, grid=(), after=(), flops=0, moved=0, scratch=()):
    count = len(args)

    def run(*refs):
        return body(*refs[:count], *refs[count + len(after) :])

    vector = pl.BlockSpec(memory_space=pltpu.VMEM)
    specs = [vector] * count if specs is None else specs
    out_specs = [vector] * len(outs) if out_specs is None else out_specs
    return pl.pallas_call(
        run,
        grid=grid,
        in_specs=[*specs, *[ANYWHERE] * len(after)],
        out_specs=out_specs,
        out_shape=[jax.ShapeDtypeStruct(shape, kind) for shape, kind in outs],
        scratch_shapes=scratch,
        compiler_params=pltpu.CompilerParams(vmem_limit_bytes=ROOM),
        cost_estimate=pl.CostEstimate(flops=flops, transcendentals=0, bytes_accessed=moved),
    )(*args, *after)


def mixed_kernel(*refs):
    out_ref = refs[-1]
    total = added(*[r[...] for r in refs[:-1]])
    frames, columns, rows, _ = out_ref.shape
    for f in range(frames):
        for c in range(columns):
            start = (f * columns + c) * rows
            out_ref[f, c] = total[start : start + rows].astype(BF16)


SCALAR = pl.BlockSpec(memory_space=pltpu.SMEM)
VECTOR = pl.BlockSpec(memory_space=pltpu.VMEM)


def hop(shift, arrays):
    return [shift(arrays[i], 1 - 2 * i, 0) for i in range(2)]


def scores_kernel(q_ref, own_ref, up_ref, down_ref, bias_ref, hot_ref, p_ref):
    qa = jnp.concatenate([q_ref[...], hot_ref[...]], axis=1)
    scores = []
    for b, ref in enumerate((up_ref, own_ref, down_ref)):
        bias = jnp.concatenate([bias_ref[0, b]] * 9, axis=0).astype(BF16)
        ka = jnp.concatenate([ref[...], bias], axis=1)
        scores.append(dot(ka, qa, ((1,), (1,))))
    top = jnp.max(scores[0], axis=0, keepdims=True)
    for s in scores[1:]:
        top = jnp.maximum(top, jnp.max(s, axis=0, keepdims=True))
    weights = [jnp.exp((s - top) * SCALE) for s in scores]
    total = jnp.sum(weights[0], axis=0, keepdims=True)
    for w in weights[1:]:
        total = total + jnp.sum(w, axis=0, keepdims=True)
    inverse = 1.0 / total
    for b in range(3):
        p_ref[0, b] = (weights[b] * inverse).astype(BF16)


def attend_kernel(p_ref, own_ref, up_ref, down_ref, perm_ref, att_ref):
    attended = None
    for b, ref in enumerate((up_ref, own_ref, down_ref)):
        part = dot(ref[...], p_ref[0, b], ((0,), (0,)))
        attended = part if attended is None else attended + part
    att_ref[...] = dot(perm_ref[...], attended.astype(BF16), ((1,), (1,))).astype(BF16)


def backward_kernel(q_ref, *refs):
    keys, values = (refs[1], refs[0], refs[2]), (refs[4], refs[3], refs[5])
    p_ref, ga_ref, perm_ref, gq_ref, gown_ref, gup_ref, gdown_ref = refs[6:]
    q = q_ref[...]
    g = dot(perm_ref[...], ga_ref[...], ((1,), (0,))).astype(BF16)
    outs = (gup_ref, gown_ref, gdown_ref)
    grads = []
    delta = None
    for b in range(3):
        gp = dot(values[b][...], g, ((1,), (1,)))
        part = jnp.sum(p_ref[0, b].astype(F32) * gp, axis=0, keepdims=True)
        delta = part if delta is None else delta + part
        grads.append(gp)
    gq = None
    for b in range(3):
        probs = p_ref[0, b]
        ds = (probs.astype(F32) * (grads[b] - delta) * SCALE).astype(BF16)
        outs[b][0] = dot(ds, q, ((1,), (0,))).astype(outs[b].dtype)
        outs[b][1] = dot(probs, g, ((1,), (0,))).astype(outs[b].dtype)
        part = dot(keys[b][...], ds, ((0,), (0,)))
        gq = part if gq is None else gq + part
    gq_ref[...] = gq.T.astype(BF16)


def total_kernel(*refs):
    out_ref = refs[-1]
    start = 0
    for i in range(0, len(refs) - 1, 3):
        part = added(refs[i][...], refs[i + 1][...], refs[i + 2][...]).astype(BF16)
        out_ref[:, :, start : start + part.shape[2]] = part
        start += part.shape[2]


def weight_kernel(order_ref, g_ref, far_g_ref, att_ref, far_att_ref, *outs):
    attended = jnp.concatenate([att_ref[...], far_att_ref[...]], axis=0)
    core = order_ref[len(outs)]
    rows = outs[0].shape[0]
    lanes = 128
    wide = -(-rows // lanes) * lanes
    for i, out_ref in enumerate(outs):
        start = order_ref[i] * (2 * rows) + core * (2 * rows - wide)
        columns = pl.ds(pl.multiple_of(start, lanes), wide)
        turned = jnp.concatenate([g_ref[:, columns].T, far_g_ref[:, columns].T], axis=1)
        turned = jnp.where(core == 0, turned[:rows], turned[wide - rows :])
        out_ref[...] = dot(turned, attended, ((1,), (0,))).astype(BF16)


STEPS = 4


def project_kernel(att_ref, w_ref, *outs):
    room = outs[0].shape[0]
    width = w_ref.shape[1] // STEPS
    for i in range(STEPS):
        columns = slice(i * width, (i + 1) * width)
        mixed = dot(att_ref[...], w_ref[:, columns], ((1,), (0,)))
        for k, out_ref in enumerate(outs):
            out_ref[:, columns] = mixed[k * room : (k + 1) * room].astype(BF16)


def attn_grad_kernel(w_ref, g_ref, ga_ref):
    width = w_ref.shape[1] // STEPS
    total = None
    for i in range(STEPS):
        columns = slice(i * width, (i + 1) * width)
        part = dot(g_ref[:, columns], w_ref[:, columns], ((1,), (1,)))
        total = part if total is None else total + part
    ga_ref[...] = total.astype(BF16)


def mask_bias(window, own_mask, seq_place, row_tiles):
    heads = window.shape[0]
    columns = own_mask.shape[0]
    rows = own_mask.reshape(columns, 3, 3, 7)[:, 1]
    query = np.arange(columns)
    delta = query[:, None] - query[None, :]
    pick = (delta[:, :, None] + REACH_W == np.arange(7)).astype(np.int32)
    bits = jnp.sum(rows.transpose(1, 0, 2)[:, None] * pick[None], axis=-1)
    dh = jnp.arange(3, dtype=jnp.int32) - 1
    tile_row = dh + seq_place
    row_ok = (tile_row >= 0) & (tile_row < row_tiles)
    inside = (jnp.abs(dh)[None, :] <= window[:, 1:2]) & row_ok[None, :] & (window[:, :1] >= 0)
    near = np.abs(delta)[None] <= window[:, 2][:, None, None]
    ok = inside[:, :, None, None] & near[:, None] & (bits > 0)[None]
    bias = jnp.where(ok, 0.0, OUTSIDE).astype(F32)
    bias = jnp.pad(bias, ((0, 0), (0, 0), (0, 0), (0, 128 - columns)))
    wide = jnp.broadcast_to(bias[:, :, :, None], (heads, 3, columns, TILE_W, 128))
    return wide.reshape(heads, 3, columns * TILE_W, 128)


def layer(queries, keys_values, out_weight, grad_out, window, block_mask):
    frames, tile_rows, columns, channels = queries.shape
    model_width = grad_out.shape[3]
    local_columns = grad_out.shape[2]
    tokens = frames * tile_rows * columns
    heads = channels // HEAD_DIM
    strips = frames * tile_rows
    row_tiles = lax.axis_size("seq")
    seq_place = lax.axis_index("seq")
    tensor_place = lax.axis_index("tensor")
    spot_z, spot_y, core = seq_place // 4, seq_place // 2 % 2, seq_place % 2
    spot_x, spot_low = tensor_place // 2, tensor_place % 2
    core = core[None].astype(jnp.int32)

    onward = [(i, i + 1) for i in range(row_tiles - 1)]
    back = [(i + 1, i) for i in range(row_tiles - 1)]
    flat_q = queries.reshape(tokens, channels)
    flat_kv = keys_values.reshape(2, tokens, channels)
    halos = []
    for i in range(2):
        up = lax.ppermute(flat_kv[i], "seq", onward)
        down = lax.ppermute(flat_kv[i], "seq", back)
        halos.append([flat_kv, up, down])

    piece = strips * local_columns
    room = -(-piece // 16) * 16
    own_grad = grad_out.transpose(0, 2, 1, 3).reshape(piece, model_width)
    own_grad = jnp.pad(own_grad, ((0, room - piece), (0, 0)))
    pieces, last_hops = gathered(own_grad, tensor_shift)
    slots = 8 * room

    row = np.arange(slots) % room
    ring, pair = (np.repeat([b[i] for b in BLOCKS], room).astype(np.int32) for i in range(2))
    owner = (spot_x + ring) % 4 * 2 + (spot_low + pair) % 2
    strip = row // (local_columns * tile_rows) * tile_rows + row % tile_rows
    place = strip * columns + owner * local_columns + row // tile_rows % local_columns
    place = jnp.where(row < piece, place, -1).astype(jnp.int32)
    cell = lax.iota(jnp.int32, tokens)
    perm = (place[:, None] == cell[None, :]).astype(BF16)
    perm_back = (cell[:, None] == place[None, :]).astype(BF16)
    hot = (cell[:, None] % columns // TILE_W == lax.iota(jnp.int32, 128)[None, :]).astype(BF16)

    own_mask = lax.dynamic_slice_in_dim(block_mask, seq_place, 1, 1).reshape(-1, OFFSETS)
    bias = mask_bias(window, own_mask, seq_place, row_tiles)

    def whole(shape):
        return pl.BlockSpec(shape, lambda h: (0,) * len(shape))

    q_spec = pl.BlockSpec((tokens, HEAD_DIM), lambda h: (0, h))
    kv_spec = pl.BlockSpec((2, tokens, HEAD_DIM), lambda h: (0, 0, h))
    key_specs = [pl.BlockSpec((None, tokens, HEAD_DIM), lambda h: (0, 0, h)), q_spec, q_spec]
    value_specs = [pl.BlockSpec((None, tokens, HEAD_DIM), lambda h: (1, 0, h)), q_spec, q_spec]
    p_spec = pl.BlockSpec((1, 3, tokens, tokens), lambda h: (h, 0, 0, 0))
    firsts = ((2, 1), (2, 0))
    others = ((1, 1), (3, 0), (3, 1), (1, 0), (0, 1), (0, 0))

    def order_of(blocks):
        ring, pair = (np.array([w[i] for w in blocks], np.int32) for i in range(2))
        chips = (spot_z + ring) % 4 * 2 + (spot_y + pair) % 2
        return jnp.concatenate([chips, core]).astype(jnp.int32)

    orders = [order_of(firsts), order_of(others)]
    pairs = heads * tokens * 3 * tokens

    (probs,) = kernel(
        scores_kernel,
        [((heads, 3, tokens, tokens), BF16)],
        [flat_q, *halos[0], bias, hot],
        [
            q_spec,
            *key_specs,
            pl.BlockSpec((1, 3, columns, 128), lambda h: (h, 0, 0, 0)),
            whole((tokens, 128)),
        ],
        [p_spec],
        grid=(heads,),
        after=[perm, perm_back, *orders],
        flops=pairs * 1000,
        moved=6 << 20,
    )
    *early, probs = lax.optimization_barrier((*pieces[:6], probs))
    all_grad = jnp.concatenate([*early, *pieces[6:]], axis=0)
    (attended,) = kernel(
        attend_kernel,
        [((slots, channels), BF16)],
        [probs, *halos[1], perm],
        [p_spec, *value_specs, whole((slots, tokens))],
        [pl.BlockSpec((slots, HEAD_DIM), lambda h: (0, h))],
        grid=(heads,),
        after=last_hops,
        flops=pairs * 500,
        moved=6 << 20,
    )
    far_grad = seq_shift(all_grad, 0, 0, 1)
    far_attended = seq_shift(attended, 0, 0, 1)

    mixed = kernel(
        project_kernel,
        [((room, model_width), BF16)] * 8,
        [attended, out_weight],
        flops=slots * model_width * channels * 3,
        moved=12 << 20,
    )
    mixed = dict(zip(BLOCKS, mixed))
    mixed_far = hop(tensor_shift, (mixed[2, 1], mixed[2, 0]))
    mixed_near = hop(tensor_shift, (mixed[1, 0], mixed[3, 1]))

    (grad_attn,) = kernel(
        attn_grad_kernel,
        [((slots, channels), BF16)],
        [out_weight, all_grad],
        after=[mixed[0, 0]],
        flops=slots * model_width * channels * 3,
        moved=12 << 20,
    )

    narrow = model_width // row_tiles

    def weight_blocks(blocks, order, after):
        return kernel(
            weight_kernel,
            [((narrow, channels), BF16)] * len(blocks),
            [order, all_grad, far_grad, attended, far_attended],
            [SCALAR] + [VECTOR] * 4,
            after=after,
            flops=slots * model_width * channels * 2 * len(blocks) // 8,
            moved=6 << 20,
        )

    weight = dict(zip(firsts, weight_blocks(firsts, orders[0], [grad_attn])))

    def differentiate(first, count, after):
        def spec(shape, at):
            def index(h):
                return tuple(h + first if i == at else 0 for i in range(len(shape)))

            return pl.BlockSpec(shape, index)

        def own(which):
            return pl.BlockSpec((None, tokens, HEAD_DIM), lambda h: (which, 0, h + first))

        width = count * HEAD_DIM
        one = spec((tokens, HEAD_DIM), 1)
        halo = ((2, tokens, width), BF16)
        return kernel(
            backward_kernel,
            [((tokens, width), BF16), (halo[0], F32), halo, halo],
            [flat_q, *halos[0], *halos[1], probs, grad_attn, perm_back],
            [
                one,
                own(0),
                one,
                one,
                own(1),
                one,
                one,
                spec((1, 3, tokens, tokens), 0),
                spec((slots, HEAD_DIM), 1),
                whole((tokens, slots)),
            ],
            [q_spec, kv_spec, kv_spec, kv_spec],
            grid=(count,),
            after=after,
            flops=pairs * 2000 * count // heads,
            moved=2 * count << 20,
        )

    def send_halo(grad_up, grad_down):
        from_below = lax.ppermute(grad_up, "seq", back)
        from_above = lax.ppermute(grad_down, "seq", onward)
        return from_below, from_above

    split = (heads + 1) // 2
    gq_a, own_a, *ends_a = differentiate(0, split, [weight[2, 1]])
    halo_a = send_halo(*ends_a)
    weight.update(zip(others, weight_blocks(others, orders[1], ends_a[:1])))
    weight_far = hop(seq_shift, (weight[2, 1], weight[2, 0]))
    weight_near = hop(seq_shift, (weight[1, 0], weight[3, 1]))

    gq_b, own_b, *ends_b = differentiate(split, heads - split, [weight[0, 0]])
    halo_b = send_halo(*ends_b)

    def relayed(kept, came, shift):
        sums = [added(k, c).astype(BF16) for k, c in zip(kept, came)]
        return hop(shift, sums)

    def side(shift, *terms):
        total = added(*terms).astype(BF16)
        return shift(total, 0, 1)

    mixed_sums = relayed((mixed[1, 1], mixed[3, 0]), mixed_far, tensor_shift)
    weight_sums = relayed((weight[1, 1], weight[3, 0]), weight_far, seq_shift)
    mixed_side = side(tensor_shift, mixed[0, 1], mixed_near[1], mixed_sums[0])
    weight_side = side(seq_shift, weight[0, 1], weight_near[1], weight_sums[0])
    (layer_out,) = kernel(
        mixed_kernel,
        [((frames, local_columns, tile_rows, model_width), BF16)],
        [mixed[0, 0], mixed_near[0], mixed_sums[1], mixed_side],
        moved=3 << 20,
    )
    grad_weight = added(weight[0, 0], weight_near[0], weight_sums[1], weight_side).astype(BF16)
    (grad_kv,) = kernel(
        total_kernel,
        [((2, tokens, channels), BF16)],
        [own_a, *halo_a, own_b, *halo_b],
        after=[layer_out],
        moved=5 << 20,
    )
    grad_q = jnp.concatenate([gq_a, gq_b], axis=1)
    return (
        layer_out.transpose(0, 2, 1, 3),
        grad_q.reshape(queries.shape),
        grad_kv.reshape(keys_values.shape),
        grad_weight.T,
    )


def solution(mesh):
    return jax.shard_map(
        layer,
        mesh=mesh,
        in_specs=(
            P(None, "seq", None, "tensor"),
            P(None, None, "seq", None, "tensor"),
            P("tensor", None),
            P(None, "seq", "tensor", None),
            P("tensor", None),
            P(),
        ),
        out_specs=(
            P(None, "seq", "tensor", None),
            P(None, "seq", None, "tensor"),
            P(None, None, "seq", None, "tensor"),
            P("tensor", "seq"),
        ),
        check_vma=False,
    )
```
